256 devices in a mesh: seq: 64 (over x, z_lo, y, core), tensor: 4 (over z_hi).
Axes of the slice: x: 4, y: 4, z: 8 (z_hi: 4, z_lo: 2; z = z_hi * 2 + z_lo), core: 2. Of those that a mesh axis runs over, the one named last changes fastest.
Arguments:
- hidden: bfloat16 [8192, 2048], P('seq'), may hold values from -6 to 6
- attn_gain: float32 [2048], replicated, may hold values from 0.1 to 1.9
- w_query: bfloat16 [2048, 1536], P(None, 'tensor'), may hold values from -0.125 to 0.125
- w_latent_down: bfloat16 [2048, 576], replicated, may hold values from -0.125 to 0.125
- kv_gain: float32 [512], replicated, may hold values from 0.1 to 1.9
- w_key_up: bfloat16 [512, 1024], P(None, 'tensor'), may hold values from -5 to 5
- w_value_up: bfloat16 [512, 1024], P(None, 'tensor'), may hold values from -2 to 2
- w_out: bfloat16 [1024, 2048], P('tensor'), may hold values from -0.1875 to 0.1875
- ffn_gain: float32 [2048], replicated, may hold values from 0.1 to 1.9
- w_gate_exp: bfloat16 [64, 2048, 1408], P('seq', None, 'tensor'), may hold values from -0.125 to 0.125
- w_up_exp: bfloat16 [64, 2048, 1408], P('seq', None, 'tensor'), may hold values from -0.125 to 0.125
- w_down_exp: bfloat16 [64, 1408, 2048], P('seq', 'tensor'), may hold values from -0.15625 to 0.15625
- page_pool: bfloat16 [64, 128, 576], P('seq'), may hold values from -6 to 6
- page_table: int32 [4, 16], replicated, may hold values from 0 to 63, as said below
- request_group: int32 [16], replicated, may hold values from 0 to 3, as said below
- suffix_lengths: int32 [16], replicated, may hold values from 1 to 2048, 8192 in all
- token_order: int32 [8192], replicated, may hold values from 0 to 8191, each once
- expert_ids: int32 [8192, 6], P('seq'), may hold values from 0 to 63, all different within a row; in each aligned block of 128 rows (0 to 127, 128 to 255, ...) at most 14 rows name the same one
- expert_gates: float32 [8192, 6], P('seq'), may hold values from 0.2 to 0.8
Outputs:
- hidden_out: bfloat16 [8192, 2048], P('seq', 'tensor')
- latent_cache: bfloat16 [8192, 576], P('seq', 'tensor')
The draws below stay inside these ranges and needn't reach their ends.
Inputs may be any that keep to these rules, and one draw needn't show every extreme that they name: `page_table`: each page id appears exactly once; row g lists the pages of group g's prefix. `request_group`: each group has exactly 4 requests. `suffix_lengths`: the lengths sum to 8192; the longest is exactly 2048. `token_order`: each concatenated position appears once. `expert_ids`: each row names 6 different experts; among the rows of one index of seq no expert is named more than 14 times, and on some indices one is named exactly 14 times.
All inputs are finite; a program needn't handle non-finite values.
Results may differ from the reference program's by a relative error of at most 0.017.
Values may be sent and summed in bfloat16 or wider, within the bound.
No kernel may reach another device: no remote copies, remote signals or barrier semaphores. Data moves between devices by JAX's collectives and lax.ppermute only.
A program may use at most 128 MiB of HBM per device.

```python
import math
import jax
import jax.numpy as jnp
import numpy as np
from jax import lax

D = 2048
HEADS = 8
NOPE = 128
ROPE = 64
VDIM = 128
LATENT = 512
FFE = 1408
TOPK = 6
GROUPS = 4
REQS = 16
PAGE = 128
TOK_DEV = 128
TOKENS = 8192
PAGES = 64
PREFIX = 2048
MOSTLEN = 2048
EXPERTS = 64
CAP = 14
N_SEQ = 64
N_TENSOR = 4


def draw_page_table(key, part):
    return jax.random.permutation(key, PAGES).astype(jnp.int32).reshape(GROUPS, PAGES // GROUPS)


def draw_request_group(key, part):
    return jax.random.permutation(key, jnp.arange(REQS, dtype=jnp.int32) % GROUPS).astype(jnp.int32)


def draw_w_key_up(key, part):
    noise_key = jax.random.fold_in(key, 21)
    return (jnp.clip(jax.random.normal(noise_key, (LATENT, HEADS * NOPE), jnp.float32), -6.0, 6.0) / NOPE ** 0.5).astype(jnp.bfloat16)


def draw_page_pool(key, part):
    shape = (PAGES, PAGE, LATENT + ROPE)
    noise_key = jax.random.fold_in(key, 31)
    return jnp.clip(jax.random.normal(noise_key, shape, jnp.float32), -6.0, 6.0).astype(jnp.bfloat16)


def level_of(own_key, shape, shards, smallest, top_value):
    def one(dim, parts):
        heights = jax.random.uniform(jax.random.fold_in(jax.random.fold_in(own_key, 6), dim), (parts,), jnp.float32, smallest / len(shards), top_value / len(shards))
        return jnp.repeat(jnp.exp(heights), shape[dim] // parts).reshape((-1,) + (1,) * (len(shape) - dim - 1))

    loudness = one(*shards[0])
    for cut in shards[1:]:
        loudness = loudness * one(*cut)
    return loudness


def length_profile(number_of, total, reach, lean):
    loads = [(1 << 20) // math.isqrt(standing ** lean) + 1 for standing in range(2, number_of + 1)]
    rest, counts = total - reach - (number_of - 1), [1] * (number_of - 1)
    while rest > 0:
        movable = [i for i in range(number_of - 1) if counts[i] < reach]
        whole, remaining = sum([loads[i] for i in movable]), rest
        for i in movable:
            more = min(reach - counts[i], max(1, remaining * loads[i] // whole), rest)
            counts[i] = counts[i] + more
            rest = rest - more
    return np.array([reach] + counts)


def uneven_parts(key, count, total, most, skew):
    if count == 2:
        one = jax.random.randint(key, (), max(1, total - most), min(most, total - 1) + 1)
        return jnp.stack([one, total - one])
    lengths = jnp.asarray(length_profile(count, total, most, skew), jnp.int32)
    twos = (count - 1) // 2
    donor, taker = lengths[1:1 + 2 * twos:2], lengths[2:2 + 2 * twos:2]
    margin = jnp.minimum(donor - 1, most - taker)
    moved = jax.random.randint(jax.random.fold_in(key, 1), (twos,), 0, 1 << 20) % (margin + 1)
    lengths = lengths.at[1:1 + 2 * twos:2].set(donor - moved).at[2:2 + 2 * twos:2].set(taker + moved)
    return lengths[jax.random.permutation(jax.random.fold_in(key, 2), count)]


def deal_out(rng, own, number, rows, count, top, most, skew):
    sequence = jax.random.permutation(rng, count)
    crowded, common = portions_of(count, rows * top, most, skew, True), portions_of(count, rows * top, most, skew, False)
    places = jnp.arange(count)

    def named(tallies, rotation):
        used = int((tallies > 0).sum())
        fixed = max(1, used // 4)
        shifted = fixed + (places - fixed + rotation * (used - fixed)) % max(1, count - fixed)
        return jnp.zeros((count,), jnp.int32).at[sequence[jnp.where(places < fixed, places, shifted)]].set(jnp.asarray(tallies, jnp.int32))

    tallies = jnp.where(number % 4 == 0, named(crowded, number // 4), named(common, number - number // 4 - 1))
    mixed = jax.random.permutation(jax.random.fold_in(own, 3), count)
    donor, taker = mixed[0:count // 2 * 2:2], mixed[1:count // 2 * 2:2]
    slack = jnp.minimum(tallies[donor] - 1, most - tallies[taker]) // 2
    slack = jnp.where((donor == sequence[0]) | (taker == sequence[0]) | (tallies[taker] == 0), 0, jnp.maximum(slack, 0))
    shifted = jax.random.randint(jax.random.fold_in(own, 4), (count // 2,), 0, 1 << 20) % (slack + 1)
    tallies = tallies.at[donor].add(-shifted).at[taker].add(shifted)
    items = jnp.searchsorted(jnp.cumsum(tallies), jnp.arange(rows * top), side="right").astype(jnp.int32)
    listing = items.reshape(top, rows).T
    listing = listing[jax.random.permutation(jax.random.fold_in(own, 1), rows)]
    rotation = jax.random.randint(jax.random.fold_in(own, 2), (rows, 1), 0, top)
    return jnp.take_along_axis(listing, (jnp.arange(top)[None, :] + rotation) % top, axis=1)


def portions_of(number_of, total, limit, skew, full):
    weights = [(1 << 20) // math.isqrt(standing ** skew) + 1 for standing in range(1, number_of + 1)]
    largest = limit if full else min(limit, max(-(-total // number_of), total * weights[0] // sum(weights)))
    least = 1 if total - largest >= number_of - 1 else 0
    given, spare = [largest] + [least] * (number_of - 1), total - largest - least * (number_of - 1)
    while spare > 0:
        free = [i for i in range(1, number_of) if given[i] < largest] or [i for i in range(1, number_of) if given[i] < limit]
        whole, remaining = sum([weights[i] for i in free]), spare
        for i in free:
            addition = min(limit - given[i], max(1, remaining * weights[i] // whole), spare)
            given[i] = given[i] + addition
            spare = spare - addition
    return np.array(given)


def scatter_about(key, dims, scale, most, cuts=(), held_as=jnp.bfloat16):
    values = scale * jax.random.normal(key, dims, jnp.float32)
    if cuts:
        values = values * level_of(key, dims, cuts, -0.22, 0.18)
    return jnp.clip(values, -most, most).astype(held_as)


def setup_inputs(seed: int = 0) -> dict:
    seeds = jax.random.split(jax.random.key(seed), 20)
    hidden = scatter_about(seeds[0], (TOKENS, D), 1.0, 6.0, ((0, 64),))
    attn_gain = jnp.clip(1.0 + 0.18 * jax.random.normal(seeds[1], (D,), jnp.float32), 0.1, 1.9)
    w_query = scatter_about(seeds[2], (D, HEADS * (NOPE + ROPE)), D ** -0.5, 0.125, ((1, 4),))
    w_latent_down = scatter_about(seeds[3], (D, LATENT + ROPE), D ** -0.5, 0.125)
    kv_gain = jnp.clip(1.0 + 0.18 * jax.random.normal(seeds[4], (LATENT,), jnp.float32), 0.1, 1.9)
    w_key_up = draw_w_key_up(jax.random.fold_in(seeds[19], 71), 0)
    w_value_up = scatter_about(seeds[6], (LATENT, HEADS * VDIM), (max(1, LATENT // 64)) ** -0.5, 2.0, ((1, 4),))
    w_out = scatter_about(seeds[7], (HEADS * VDIM, D), (HEADS * VDIM) ** -0.5, 0.1875, ((0, 4),))
    ffn_gain = jnp.clip(1.0 + 0.18 * jax.random.normal(seeds[8], (D,), jnp.float32), 0.1, 1.9)
    w_gate_exp = scatter_about(seeds[9], (EXPERTS, D, FFE), D ** -0.5, 0.125, ((0, 64), (2, 4)))
    w_up_exp = scatter_about(seeds[10], (EXPERTS, D, FFE), D ** -0.5, 0.125, ((0, 64), (2, 4)))
    w_down_exp = scatter_about(seeds[11], (EXPERTS, FFE, D), FFE ** -0.5, 0.15625, ((0, 64), (1, 4)))
    page_pool = draw_page_pool(jax.random.fold_in(seeds[19], 71), 0)
    page_table = draw_page_table(jax.random.fold_in(seeds[19], 71), 0)
    request_group = draw_request_group(jax.random.fold_in(seeds[19], 71), 0)
    suffix_lengths = uneven_parts(seeds[15], REQS, TOKENS, MOSTLEN, 2).astype(jnp.int32)
    token_order = jax.random.permutation(seeds[16], TOKENS).astype(jnp.int32)
    expert_ids_keys = jax.random.split(jax.random.fold_in(seeds[17], 1), TOKENS // TOK_DEV)
    expert_ids_turns = jax.random.permutation(jax.random.fold_in(seeds[17], 3), TOKENS // TOK_DEV)
    expert_ids = jax.vmap(lambda own, number: deal_out(jax.random.fold_in(seeds[17], 2), own, number, TOK_DEV, EXPERTS, TOPK, CAP, 1))(expert_ids_keys, expert_ids_turns).reshape((TOKENS, TOPK))
    expert_gates = jnp.clip(0.2 + 0.6 * jax.random.uniform(seeds[18], (TOKENS, TOPK), jnp.float32) ** level_of(seeds[18], (TOKENS, TOPK), ((0, 64),), -0.2, 0.2), 0.2, 0.8)
    return dict(hidden=hidden, attn_gain=attn_gain, w_query=w_query, w_latent_down=w_latent_down, kv_gain=kv_gain, w_key_up=w_key_up, w_value_up=w_value_up, w_out=w_out, ffn_gain=ffn_gain, w_gate_exp=w_gate_exp, w_up_exp=w_up_exp, w_down_exp=w_down_exp, page_pool=page_pool, page_table=page_table, request_group=request_group, suffix_lengths=suffix_lengths, token_order=token_order, expert_ids=expert_ids, expert_gates=expert_gates)


EPSILON = 1e-06
ROPE_BASE = 50000.0
MASKED_SCORE = -1e+30

def rms_scale(values, gain):
    return values * lax.rsqrt(lax.optimization_barrier(jnp.mean(values * values, axis=-1, keepdims=True)) + EPSILON) * gain

def rotate(values, position):
    half_width = values.shape[-1] // 2
    frequency = ROPE_BASE ** (-2.0 * jnp.arange(half_width, dtype=jnp.float32) / values.shape[-1])
    angles = position[..., None] * frequency
    angle_cos = jnp.cos(angles)
    angle_sin = jnp.sin(angles)
    first_half = values[..., :half_width]
    second_half = values[..., half_width:]
    return jnp.concatenate([first_half * angle_cos - second_half * angle_sin, second_half * angle_cos + first_half * angle_sin], axis=-1)

def token_meta(token_order, suffix_lengths, request_group):
    ends = jnp.cumsum(suffix_lengths).astype(jnp.int32)
    starts = (ends - suffix_lengths).astype(jnp.int32)
    request = lax.optimization_barrier(jnp.sum((token_order[:, None] >= ends[None, :]).astype(jnp.int32), axis=1)).astype(jnp.int32)
    onehot = request[:, None] == jnp.arange(suffix_lengths.shape[0], dtype=jnp.int32)[None, :]
    offset = (token_order - lax.optimization_barrier(jnp.sum(jnp.where(onehot, starts[None, :], 0), axis=1))).astype(jnp.int32)
    group = lax.optimization_barrier(jnp.sum(jnp.where(onehot, request_group[None, :], 0), axis=1)).astype(jnp.int32)
    return (request, offset, group)

def page_groups(page_table, pages):
    hits = page_table[:, :, None] == jnp.arange(pages, dtype=jnp.int32)[None, None, :]
    labels = jnp.arange(page_table.shape[0], dtype=jnp.int32)[:, None, None]
    return lax.optimization_barrier(jnp.sum(jnp.where(hits, labels, 0), axis=(0, 1))).astype(jnp.int32)

def reference(hidden, attn_gain, w_query, w_latent_down, kv_gain, w_key_up, w_value_up, w_out, ffn_gain, w_gate_exp, w_up_exp, w_down_exp, page_pool, page_table, request_group, suffix_lengths, token_order, expert_ids, expert_gates):
    request, offset, group = token_meta(token_order, suffix_lengths, request_group)
    position = (PREFIX + offset).astype(jnp.float32)
    normed = rms_scale(hidden.astype(jnp.float32), attn_gain.astype(jnp.float32)).astype(jnp.bfloat16)
    query = jnp.dot(normed, w_query, preferred_element_type=jnp.float32).astype(jnp.bfloat16).reshape(TOKENS, HEADS, NOPE + ROPE)
    key_up = w_key_up.astype(jnp.float32).reshape(LATENT, HEADS, NOPE)
    query_latent = jnp.einsum('thd,lhd->thl', query[..., :NOPE].astype(jnp.float32), key_up).astype(jnp.bfloat16)
    query_rope = rotate(query[..., NOPE:].astype(jnp.float32), position[:, None]).astype(jnp.bfloat16)
    raw_latent = jnp.dot(normed, w_latent_down, preferred_element_type=jnp.float32)
    latent = rms_scale(raw_latent[:, :LATENT], kv_gain.astype(jnp.float32))
    key_rope = rotate(raw_latent[:, LATENT:], position)
    latent_cache = jnp.concatenate([latent, key_rope], axis=1).astype(jnp.bfloat16)
    page_group = page_groups(page_table, PAGES)
    all_keys = jnp.concatenate([page_pool.reshape(PAGES * PAGE, LATENT + ROPE), latent_cache], axis=0).astype(jnp.float32)
    minus_pages = jnp.full((PAGES * PAGE,), -1, jnp.int32)
    minus_tokens = jnp.full((TOKENS,), -1, jnp.int32)
    key_group = jnp.concatenate([jnp.repeat(page_group, PAGE), minus_tokens])
    key_request = jnp.concatenate([minus_pages, request])
    key_offset = jnp.concatenate([minus_pages, offset])
    scale = (NOPE + ROPE) ** (-0.5)
    value_up = w_value_up.astype(jnp.float32).reshape(LATENT, HEADS, VDIM)

    def attend(block):
        block_latent, block_rope, block_group, block_request, block_offset = block
        scores = (jnp.einsum('qhl,kl->qhk', block_latent.astype(jnp.float32), all_keys[:, :LATENT]) + jnp.einsum('qhr,kr->qhk', block_rope.astype(jnp.float32), all_keys[:, LATENT:])) * scale
        visible = (key_group[None, :] == block_group[:, None]) | (key_request[None, :] == block_request[:, None]) & (key_offset[None, :] <= block_offset[:, None])
        visible = visible[:, None, :]
        row_max = lax.optimization_barrier(jnp.max(jnp.where(visible, scores, MASKED_SCORE), axis=-1, keepdims=True))
        weights = jnp.where(visible, jnp.exp(scores - row_max), 0.0)
        denominator = lax.optimization_barrier(jnp.sum(weights, axis=-1))
        rounded = lax.optimization_barrier(weights.astype(jnp.bfloat16)).astype(jnp.float32)
        summed = jnp.einsum('qhk,kl->qhl', rounded, all_keys[:, :LATENT])
        attended = (summed / denominator[..., None]).astype(jnp.bfloat16)
        head_values = jnp.einsum('qhl,lhd->qhd', attended.astype(jnp.float32), value_up).astype(jnp.bfloat16)
        return jnp.dot(head_values.reshape(head_values.shape[0], HEADS * VDIM), w_out, preferred_element_type=jnp.float32)
    blocks = (query_latent.reshape(N_SEQ, TOK_DEV, HEADS, LATENT), query_rope.reshape(N_SEQ, TOK_DEV, HEADS, ROPE), group.reshape(N_SEQ, TOK_DEV), request.reshape(N_SEQ, TOK_DEV), offset.reshape(N_SEQ, TOK_DEV))
    attention = lax.map(attend, blocks).reshape(TOKENS, D)
    mixed = (hidden.astype(jnp.float32) + attention).astype(jnp.bfloat16)
    ffn_input = rms_scale(mixed.astype(jnp.float32), ffn_gain.astype(jnp.float32)).astype(jnp.bfloat16)
    flat_ids = expert_ids.reshape(N_SEQ, TOK_DEV * TOPK)
    onehot = (flat_ids[..., None] == jnp.arange(EXPERTS, dtype=jnp.int32)[None, None, :]).astype(jnp.int32)
    slot_index = lax.optimization_barrier(jnp.sum((jnp.cumsum(onehot, axis=1) - onehot) * onehot, axis=2)).astype(jnp.int32)
    sources = jnp.broadcast_to(jnp.arange(N_SEQ, dtype=jnp.int32)[:, None], flat_ids.shape)
    token_index = (sources * TOK_DEV + jnp.arange(TOK_DEV * TOPK, dtype=jnp.int32)[None, :] // TOPK).astype(jnp.int32)
    row_table = jnp.full((EXPERTS, N_SEQ, CAP), TOKENS, jnp.int32).at[flat_ids, sources, slot_index].set(token_index)
    gate_table = jnp.zeros((EXPERTS, N_SEQ, CAP), jnp.float32).at[flat_ids, sources, slot_index].set(expert_gates.reshape(N_SEQ, TOK_DEV * TOPK).astype(jnp.float32))
    padded_input = jnp.concatenate([ffn_input, jnp.zeros((1, D), jnp.bfloat16)], axis=0)

    def expert_step(totals, inputs):
        rows_index, row_gates, gate_weight, up_weight, down_weight = inputs
        chosen = padded_input[rows_index]
        gate_proj = jnp.dot(chosen, gate_weight, preferred_element_type=jnp.float32)
        up_proj = jnp.dot(chosen, up_weight, preferred_element_type=jnp.float32)
        activated = (jax.nn.silu(gate_proj) * up_proj).astype(jnp.bfloat16)
        split_act = activated.reshape(-1, N_TENSOR, FFE // N_TENSOR).astype(jnp.float32)
        split_down = down_weight.reshape(N_TENSOR, FFE // N_TENSOR, D).astype(jnp.float32)
        quarters = jnp.einsum('nqf,qfd->qnd', split_act, split_down)
        quarters = lax.optimization_barrier(quarters.astype(jnp.bfloat16)).astype(jnp.float32)
        result = lax.optimization_barrier(jnp.sum(quarters, axis=0)) * row_gates[:, None]
        return (totals.at[rows_index].add(result), None)
    totals, _ = lax.scan(expert_step, jnp.zeros((TOKENS + 1, D), jnp.float32), (row_table.reshape(EXPERTS, N_SEQ * CAP), gate_table.reshape(EXPERTS, N_SEQ * CAP), w_gate_exp, w_up_exp, w_down_exp))
    hidden_out = (mixed.astype(jnp.float32) + totals[:TOKENS]).astype(jnp.bfloat16)
    return (hidden_out, latent_cache)
```

```python
import functools

import jax
import jax.numpy as jnp
import numpy as np
from jax import lax
from jax.experimental import pallas as pl
from jax.experimental.pallas import tpu as pltpu
from jax.sharding import PartitionSpec as P

NOPE = 128
ROPE = 64
VDIM = 128
LATENT = 512
KEY = LATENT + ROPE
SLOTS = 16
EPSILON = 1e-06
ROPE_BASE = 50000.0
MASKED = -1e30

NX, NZ, NY, NC = 4, 2, 4, 2
BF = jnp.bfloat16
F32 = jnp.float32
VM = pltpu.MemorySpace.VMEM
SM = pltpu.MemorySpace.SMEM


def seq_id(x, z, y, c):
    return (((x % NX) * NZ + z % NZ) * NY + y % NY) * NC + c % NC


def seq_perm(dx, dz, dy, dc):
    pairs = []
    for x in range(NX):
        for z in range(NZ):
            for y in range(NY):
                for c in range(NC):
                    pairs.append((seq_id(x + dx, z + dz, y + dy, c + dc), seq_id(x, z, y, c)))
    return pairs


def tensor_from(d, n):
    return [((t + d) % n, t) for t in range(n)]


def zy_groups():
    return [
        [seq_id(x, z, y, c) for z in range(NZ) for y in range(NY)]
        for x in range(NX)
        for c in range(NC)
    ]


def my_place():
    s = lax.axis_index("seq")
    c = lax.rem(s, NC)
    y = lax.rem(lax.div(s, NC), NY)
    z = lax.rem(lax.div(s, NC * NY), NZ)
    x = lax.div(s, NC * NY * NZ)
    return x, z, y, c


def dot(a, b, dims=(((1,), (0,)), ((), ()))):
    return lax.dot_general(a, b, dims, preferred_element_type=F32)


def token_rows(tok, lengths, group):
    tok = tok.astype(F32)
    start = jnp.zeros_like(tok)
    grp = jnp.zeros_like(tok)
    end = jnp.int32(0)
    for r in range(lengths.shape[0]):
        begin = end
        end = end + lengths[r]
        ef = end.astype(F32)
        bf = begin.astype(F32)
        past = tok >= ef
        start = jnp.where(past, ef, start)
        if group is not None:
            inside = jnp.logical_and(tok >= bf, tok < ef)
            grp = jnp.where(inside, group[r].astype(F32), grp)
    return tok, start, grp


def to_columns(rows, n):
    which = lax.broadcasted_iota(jnp.int32, (n, n), 0)
    out = jnp.zeros((n, n), F32)
    for i, row in enumerate(rows):
        out = jnp.where(which == i, jnp.broadcast_to(row, (n, n)), out)
    return out.T


def project_kernel(prefix, lengths, tok_ref, freq_ref, hid_ref, gain_ref, wq_ref, wl_ref, kvg_ref, q_ref, lat_ref):
    n = hid_ref.shape[0]
    s = lax.axis_index("seq")
    tok, start, _ = token_rows(tok_ref[pl.ds(s, 1), :], lengths, None)
    position = to_columns([tok - start + float(prefix)], n)[:, 0:1]
    angles = position * freq_ref[...]
    lane = lax.broadcasted_iota(jnp.int32, (n, 128), 1)
    first = lax.rem(lane, ROPE) < ROPE // 2
    cos = jnp.cos(angles)
    sin = jnp.where(first, -jnp.sin(angles), jnp.sin(angles))

    def rotate(v):
        partner = jnp.where(first, pltpu.roll(v, 128 - ROPE // 2, 1), pltpu.roll(v, ROPE // 2, 1))
        return v * cos + partner * sin

    hid = hid_ref[...].astype(F32)
    scale = lax.rsqrt(jnp.mean(hid * hid, axis=-1, keepdims=True) + EPSILON)
    normed = (hid * scale * gain_ref[...]).astype(BF)
    query = dot(normed, wq_ref[...]).astype(BF)
    width = NOPE + ROPE
    pe = jnp.concatenate([query[:, NOPE:width], query[:, width + NOPE : 2 * width]], axis=1)
    q_ref[:, 0:128] = query[:, 0:NOPE]
    q_ref[:, 128:256] = query[:, width : width + NOPE]
    q_ref[:, 256:384] = rotate(pe.astype(F32)).astype(BF)
    raw = dot(normed, wl_ref[...])
    lat = raw[:, :LATENT]
    lscale = lax.rsqrt(jnp.mean(lat * lat, axis=-1, keepdims=True) + EPSILON)
    lat_ref[:, :LATENT] = (lat * lscale * kvg_ref[...]).astype(BF)
    pe = raw[:, LATENT:]
    lat_ref[:, LATENT:] = rotate(jnp.concatenate([pe, pe], axis=1))[:, :ROPE].astype(BF)


def attend_kernel(
    place, lengths, group, table, tok_ref, q_ref, pa_ref, pb_ref, la_ref, lb_ref, ku_ref, vu_ref,
    out_ref, s_ref, qf_ref, owner,
):
    j = pl.program_id(0)
    n = q_ref.shape[1]
    x, z, y, c = place[0], place[1], place[2], place[3]

    @pl.when(j == 0)
    def _():
        for g in range(table.shape[0]):
            for i in range(table.shape[1]):
                owner[table[g, i]] = g

    me = seq_id(x, z + lax.div(j, NY), y + lax.rem(j, NY), c)
    tok, start, grp = token_rows(tok_ref[pl.ds(me, 1), :], lengths, group)
    cols = to_columns([tok, start, grp], n)
    two = jnp.concatenate([cols, cols], axis=0)
    pos_q, start_q, grp_q = two[:, 0:1], two[:, 1:2], two[:, 2:3]

    for h in range(2):
        up = ku_ref[:, h * NOPE : (h + 1) * NOPE]
        nope = q_ref[0, :, h * NOPE : (h + 1) * NOPE]
        qf_ref[h * n : (h + 1) * n, :LATENT] = dot(nope, up, (((1,), (1,)), ((), ()))).astype(BF)
        qf_ref[h * n : (h + 1) * n, LATENT:] = q_ref[0, :, 2 * NOPE + h * ROPE : 2 * NOPE + (h + 1) * ROPE]
    qf = qf_ref[...]
    keys = (pa_ref, pb_ref, la_ref, lb_ref)
    high = jnp.full((2 * n, 1), MASKED, F32)
    for b, k_ref in enumerate(keys):
        sc = dot(qf, k_ref[...], (((1,), (1,)), ((), ())))
        for i in range(NX):
            holder = seq_id(x + i, z, y, c + b % 2)
            part = sc[:, i * n : (i + 1) * n]
            if b < 2:
                bias = jnp.where(grp_q == owner[holder].astype(F32), 0.0, MASKED)
                part = part + bias
            else:
                pos_k = tok_ref[pl.ds(holder, 1), :].astype(F32)
                seen = jnp.logical_and(pos_k >= start_q, pos_k <= pos_q)
                part = jnp.where(seen, part, MASKED)
            s_ref[:, (b * NX + i) * n : (b * NX + i + 1) * n] = part
            high = jnp.maximum(high, jnp.max(part, axis=-1, keepdims=True))
    scale = (NOPE + ROPE) ** (-0.5)
    log2e = 1.4426950408889634
    top = jnp.where(high > 0.5 * MASKED, high, 0.0)
    den = jnp.zeros((2 * n, 1), F32)
    acc = jnp.zeros((2 * n, LATENT), F32)
    width = NX * n
    for b, k_ref in enumerate(keys):
        w = jnp.exp2((s_ref[:, b * width : (b + 1) * width] - top) * (scale * log2e))
        den = den + jnp.sum(w, axis=-1, keepdims=True)
        acc = acc + dot(w.astype(BF), k_ref[:, :LATENT])
    some = den > 0.0
    att = (acc / jnp.where(some, den, 1.0)).astype(BF)
    lse = jnp.where(some, top * scale + jnp.log(jnp.where(some, den, 1.0)), MASKED)
    hi = lse.astype(BF).astype(F32)
    mid = (lse - hi).astype(BF).astype(F32)
    low = lse - hi - mid
    lane = lax.broadcasted_iota(jnp.int32, (n, 128), 1)
    stat = jnp.zeros((n, 128), F32)
    for h in range(2):
        rows = slice(h * n, (h + 1) * n)
        out_ref[0, :, h * VDIM : (h + 1) * VDIM] = dot(
            att[rows], vu_ref[:, h * VDIM : (h + 1) * VDIM]
        ).astype(BF)
        for i, term in enumerate((hi, mid, low)):
            stat = jnp.where(lane == 3 * h + i, term[rows], stat)
    out_ref[0, :, 2 * VDIM :] = stat.astype(BF)


def project_out_kernel(got_ref, wo_ref, *outs):
    t = lax.axis_index("tensor")
    m = got_ref.shape[0]
    vals = []
    for h in range(2):
        lse = []
        for i in range(m):
            st = got_ref[i, :, 2 * VDIM :].astype(F32)
            lse.append(st[:, 3 * h : 3 * h + 1] + st[:, 3 * h + 1 : 3 * h + 2] + st[:, 3 * h + 2 : 3 * h + 3])
        top = functools.reduce(jnp.maximum, lse)
        den = jnp.zeros_like(top)
        acc = jnp.zeros((got_ref.shape[1], VDIM), F32)
        for i in range(m):
            w = jnp.exp(lse[i] - top)
            den = den + w
            acc = acc + w * got_ref[i, :, h * VDIM : (h + 1) * VDIM].astype(F32)
        vals.append((acc / den).astype(BF))
    vals = jnp.concatenate(vals, axis=1)
    q = outs[0].shape[1]
    for j, out in enumerate(outs):
        col = pl.multiple_of(lax.rem(t + j, len(outs)) * q, q)
        out[...] = dot(vals, wo_ref[:, pl.ds(col, q)]).astype(BF)


def mix_kernel(hid_ref, a_ref, b_ref, c_ref, d_ref, out_ref):
    t = lax.axis_index("tensor")
    q = out_ref.shape[1]
    col = pl.multiple_of(t * q, q)
    total = a_ref[...].astype(F32) + b_ref[...].astype(F32) + c_ref[...].astype(F32) + d_ref[...].astype(F32)
    out_ref[...] = (hid_ref[:, pl.ds(col, q)].astype(F32) + total).astype(BF)


def finish_kernel(mix_ref, a_ref, b_ref, c_ref, d_ref, out_ref):
    total = a_ref[...].astype(F32) + b_ref[...].astype(F32) + c_ref[...].astype(F32) + d_ref[...].astype(F32)
    out_ref[...] = (mix_ref[...].astype(F32) + total).astype(BF)


def slots_kernel(ids_ref, gates_ref, oh_ref, hi_ref, lo_ref):
    experts = oh_ref.shape[0] // SLOTS
    n = oh_ref.shape[1]
    which = lax.broadcasted_iota(jnp.int32, (experts, n), 0)
    named = jnp.zeros((experts, n), F32)
    gate = jnp.zeros((experts, n), F32)
    for k in range(ids_ref.shape[0]):
        hit = which == ids_ref[k : k + 1, :]
        named = jnp.where(hit, 1.0, named)
        gate = jnp.where(hit, gates_ref[k : k + 1, :], gate)
    before = lax.broadcasted_iota(jnp.int32, (n, n), 0) < lax.broadcasted_iota(jnp.int32, (n, n), 1)
    count = dot(named.astype(BF), jnp.where(before, 1.0, 0.0).astype(BF))
    slot = jnp.where(named > 0.0, count, -1.0)
    ghi = gate.astype(BF).astype(F32)
    glo = gate - ghi
    level = lax.broadcasted_iota(jnp.int32, (SLOTS, n), 0).astype(F32)
    for e in range(experts):
        hit = slot[e : e + 1, :] == level
        rows = slice(e * SLOTS, (e + 1) * SLOTS)
        oh_ref[rows, :] = jnp.where(hit, 1.0, 0.0).astype(BF)
        hi_ref[rows, :] = jnp.where(hit, ghi[e : e + 1, :], 0.0).astype(BF)
        lo_ref[rows, :] = jnp.where(hit, glo[e : e + 1, :], 0.0).astype(BF)


def dispatch_kernel(a_ref, b_ref, c_ref, d_ref, gain_ref, oh_ref, out_ref, in_ref):
    parts = (a_ref, b_ref, c_ref, d_ref)
    q = a_ref.shape[1]
    t = lax.axis_index("tensor")

    @pl.when(pl.program_id(0) == 0)
    def _():
        sq = jnp.zeros((a_ref.shape[0], 1), F32)
        for p in parts:
            v = p[...].astype(F32)
            sq = sq + jnp.sum(v * v, axis=-1, keepdims=True)
        scale = lax.rsqrt(sq / (q * len(parts)) + EPSILON)
        for j, p in enumerate(parts):
            col = pl.multiple_of(lax.rem(t + j, len(parts)) * q, q)
            in_ref[:, pl.ds(col, q)] = (p[...].astype(F32) * scale * gain_ref[:, pl.ds(col, q)]).astype(BF)

    out_ref[...] = dot(oh_ref[...], in_ref[...]).astype(BF)


def expert_kernel(x_ref, wg_ref, wu_ref, wd_ref, out_ref):
    x = x_ref[...]
    gate = dot(x, wg_ref[...])
    up = dot(x, wu_ref[...])
    act = (gate / (1.0 + jnp.exp(-gate)) * up).astype(BF)
    out_ref[...] = dot(act, wd_ref[...]).astype(BF)


def combine_kernel(rows_ref, hi_ref, lo_ref, *outs):
    t = lax.axis_index("tensor")
    q = outs[0].shape[1]
    tn = (((0,), (0,)), ((), ()))
    for j, out in enumerate(outs):
        col = pl.multiple_of(lax.rem(t + j, len(outs)) * q, q)
        rows = rows_ref[:, pl.ds(col, q)]
        out[...] = (dot(hi_ref[...], rows, tn) + dot(lo_ref[...], rows, tn)).astype(BF)


def whole(n):
    return [pl.BlockSpec(memory_space=VM)] * n


def local(
    hidden, attn_gain, w_query, w_latent_down, kv_gain, w_key_up, w_value_up, w_out, ffn_gain,
    w_gate_exp, w_up_exp, w_down_exp, page_pool, page_table, request_group, suffix_lengths,
    token_order, expert_ids, expert_gates,
):
    seq_count = lax.axis_size("seq")
    tensor_count = lax.axis_size("tensor")
    tensor_index = lax.axis_index("tensor")
    n, d = hidden.shape
    quarter = d // tensor_count
    prefix = page_table.shape[1] * page_pool.shape[1]
    tok = token_order.reshape(seq_count, n)
    place = jnp.stack(my_place()).astype(jnp.int32)
    params = pltpu.CompilerParams(vmem_limit_bytes=56 << 20)

    def spread(piece):
        got = [lax.ppermute(piece, "seq", seq_perm(i, 0, 0, 0)) for i in range(1, NX)]
        own = jnp.concatenate([piece] + got, axis=0)
        return own, lax.ppermute(own, "seq", seq_perm(0, 0, 0, 1))

    pages_a, pages_b = spread(page_pool[0])

    freq = ROPE_BASE ** (-2.0 * np.arange(ROPE // 2, dtype=np.float64) / ROPE)
    freq = jnp.asarray(np.tile(freq, 4)[None, :], F32)
    query, latent_cache = pl.pallas_call(
        functools.partial(project_kernel, prefix),
        out_shape=(
            jax.ShapeDtypeStruct((n, w_query.shape[1]), BF),
            jax.ShapeDtypeStruct((n, KEY), BF),
        ),
        in_specs=[pl.BlockSpec(memory_space=SM)] + whole(7),
        out_specs=tuple(whole(2)),
        compiler_params=params,
        name="project",
    )(suffix_lengths, tok, freq, hidden, attn_gain.reshape(1, d), w_query, w_latent_down, kv_gain.reshape(1, LATENT))

    lat_a, lat_b = spread(latent_cache)
    peers = [(i // NY, i % NY) for i in range(NZ * NY)]
    queries = jnp.stack(
        [query if i == 0 else lax.ppermute(query, "seq", seq_perm(0, dz, dy, 0)) for i, (dz, dy) in enumerate(peers)]
    )

    oh, ghi, glo = pl.pallas_call(
        slots_kernel,
        out_shape=(jax.ShapeDtypeStruct((seq_count * SLOTS, n), BF),) * 3,
        in_specs=whole(2),
        out_specs=tuple(whole(3)),
        compiler_params=params,
        name="slots",
    )(expert_ids.T, expert_gates.T)

    m = len(peers)
    keys = NX * n

    def place_of(j, place, *_):
        return (lax.rem(place[1] + lax.div(j, NY), NZ) * NY + lax.rem(place[2] + lax.rem(j, NY), NY), 0, 0)

    def fixed(shape):
        return pl.BlockSpec(shape, lambda j, *_: (0,) * len(shape))

    partial = pl.pallas_call(
        attend_kernel,
        out_shape=jax.ShapeDtypeStruct((m, n, 3 * VDIM), BF),
        grid_spec=pltpu.PrefetchScalarGridSpec(
            num_scalar_prefetch=4,
            grid=(m,),
            in_specs=[
                fixed(tok.shape),
                pl.BlockSpec((1, n, query.shape[1]), lambda j, *_: (j, 0, 0)),
                fixed((keys, KEY)),
                fixed((keys, KEY)),
                fixed((keys, KEY)),
                fixed((keys, KEY)),
                fixed(w_key_up.shape),
                fixed(w_value_up.shape),
            ],
            out_specs=pl.BlockSpec((1, n, 3 * VDIM), place_of),
            scratch_shapes=[
                pltpu.VMEM((2 * n, 4 * keys), F32),
                pltpu.VMEM((2 * n, KEY), BF),
                pltpu.SMEM((seq_count,), jnp.int32),
            ],
        ),
        compiler_params=params,
        name="attend",
    )(place, suffix_lengths, request_group, page_table, tok, queries, pages_a, pages_b, lat_a, lat_b, w_key_up, w_value_up)

    got = lax.all_to_all(partial, "seq", 0, 0, tiled=True, axis_index_groups=zy_groups())

    piece = jax.ShapeDtypeStruct((n, quarter), BF)

    def exchange(parts):
        return [parts[0]] + [
            lax.ppermute(parts[j], "tensor", tensor_from(-j, tensor_count)) for j in range(1, tensor_count)
        ]

    heads = pl.pallas_call(
        project_out_kernel,
        out_shape=(piece,) * tensor_count,
        in_specs=whole(2),
        out_specs=tuple(whole(tensor_count)),
        compiler_params=params,
        name="project_out",
    )(got, w_out)
    mixed = pl.pallas_call(
        mix_kernel, out_shape=piece, in_specs=whole(5), out_specs=whole(1)[0], compiler_params=params, name="mix"
    )(hidden, *exchange(heads))
    mixed_all = [mixed] + [
        lax.ppermute(mixed, "tensor", tensor_from(j, tensor_count)) for j in range(1, tensor_count)
    ]
    rows = seq_count * SLOTS
    block = rows // 4
    outbound = pl.pallas_call(
        dispatch_kernel,
        out_shape=jax.ShapeDtypeStruct((rows, d), BF),
        grid=(rows // block,),
        in_specs=[pl.BlockSpec((n, quarter), lambda i: (0, 0))] * 4
        + [pl.BlockSpec((1, d), lambda i: (0, 0)), pl.BlockSpec((block, n), lambda i: (i, 0))],
        out_specs=pl.BlockSpec((block, d), lambda i: (i, 0)),
        scratch_shapes=[pltpu.VMEM((n, d), BF)],
        compiler_params=params,
        name="dispatch",
    )(*mixed_all, ffn_gain.reshape(1, d), oh)
    arrived = lax.all_to_all(outbound.reshape(seq_count, SLOTS, d), "seq", 0, 0, tiled=True)
    hid = w_gate_exp.shape[2]
    results = pl.pallas_call(
        expert_kernel,
        out_shape=jax.ShapeDtypeStruct((rows, d), BF),
        grid=(rows // block,),
        in_specs=[
            pl.BlockSpec((block, d), lambda i: (i, 0)),
            pl.BlockSpec((d, hid), lambda i: (0, 0)),
            pl.BlockSpec((d, hid), lambda i: (0, 0)),
            pl.BlockSpec((hid, d), lambda i: (0, 0)),
        ],
        out_specs=pl.BlockSpec((block, d), lambda i: (i, 0)),
        compiler_params=params,
        name="expert",
    )(arrived.reshape(rows, d), w_gate_exp[0], w_up_exp[0], w_down_exp[0])
    back = lax.all_to_all(results.reshape(seq_count, SLOTS, d), "seq", 0, 0, tiled=True)
    sums = pl.pallas_call(
        combine_kernel,
        out_shape=(piece,) * tensor_count,
        in_specs=whole(3),
        out_specs=tuple(whole(tensor_count)),
        compiler_params=params,
        name="combine",
    )(back.reshape(rows, d), ghi, glo)
    hidden_out = pl.pallas_call(
        finish_kernel, out_shape=piece, in_specs=whole(5), out_specs=whole(1)[0], compiler_params=params, name="finish"
    )(mixed, *exchange(sums))
    width = KEY // tensor_count
    cache_part = lax.dynamic_slice_in_dim(latent_cache, tensor_index * width, width, 1)
    return (hidden_out, cache_part)


def solution(mesh):
    placed = (
        P("seq", None),
        P(),
        P(None, "tensor"),
        P(),
        P(),
        P(None, "tensor"),
        P(None, "tensor"),
        P("tensor", None),
        P(),
        P("seq", None, "tensor"),
        P("seq", None, "tensor"),
        P("seq", "tensor", None),
        P("seq", None, None),
        P(),
        P(),
        P(),
        P(),
        P("seq", None),
        P("seq", None),
    )
    return jax.shard_map(
        local,
        mesh=mesh,
        in_specs=placed,
        out_specs=(P("seq", "tensor"), P("seq", "tensor")),
        check_vma=False,
    )
```

```python
import functools

import jax
import jax.numpy as jnp
import numpy as np
from jax import lax
from jax.experimental import pallas as pl
from jax.experimental.pallas import tpu as pltpu
from jax.sharding import PartitionSpec as P


NOPE = 128
ROPE = 64
VDIM = 128
LATENT = 512
KEY = LATENT + ROPE
SLOTS = 16
EPSILON = 1e-06
ROPE_BASE = 50000.0
MASKED = -1e30

NX, NZ, NY, NC = 4, 2, 4, 2
BF = jnp.bfloat16
F32 = jnp.float32
NT = (((1,), (1,)), ((), ()))
VM = pltpu.MemorySpace.VMEM
SM = pltpu.MemorySpace.SMEM


def seq_id(x, z, y, c):
    return (((x % NX) * NZ + z % NZ) * NY + y % NY) * NC + c % NC


def seq_perm(dx, dz, dy, dc):
    pairs = []
    for x in range(NX):
        for z in range(NZ):
            for y in range(NY):
                for c in range(NC):
                    pairs.append((seq_id(x + dx, z + dz, y + dy, c + dc), seq_id(x, z, y, c)))
    return pairs


def tensor_from(d, n):
    return [((t + d) % n, t) for t in range(n)]


def zy_groups():
    return [
        [seq_id(x, z, y, c) for z in range(NZ) for y in range(NY)]
        for x in range(NX)
        for c in range(NC)
    ]


def my_place():
    s = lax.axis_index("seq")
    c = lax.rem(s, NC)
    y = lax.rem(lax.div(s, NC), NY)
    z = lax.rem(lax.div(s, NC * NY), NZ)
    x = lax.div(s, NC * NY * NZ)
    return x, z, y, c


def dot(a, b, dims=(((1,), (0,)), ((), ()))):
    return lax.dot_general(a, b, dims, preferred_element_type=F32)


def token_rows(tok, lengths, group):
    tok = tok.astype(F32)
    start = jnp.zeros_like(tok)
    grp = jnp.zeros_like(tok)
    end = jnp.int32(0)
    for r in range(lengths.shape[0]):
        begin = end
        end = end + lengths[r]
        ef = end.astype(F32)
        bf = begin.astype(F32)
        past = tok >= ef
        start = jnp.where(past, ef, start)
        if group is not None:
            inside = jnp.logical_and(tok >= bf, tok < ef)
            grp = jnp.where(inside, group[r].astype(F32), grp)
    return tok, start, grp


def to_columns(rows, n):
    which = lax.broadcasted_iota(jnp.int32, (n, n), 0)
    out = jnp.zeros((n, n), F32)
    for i, row in enumerate(rows):
        out = jnp.where(which == i, jnp.broadcast_to(row, (n, n)), out)
    return out.T


def project_kernel(prefix, lengths, tok_ref, fcol_ref, frow_ref, hid_ref, gain_ref, wq_ref, wl_ref, kvg_ref, q_ref, lat_ref):
    n = hid_ref.shape[0]
    half = ROPE // 2
    s = lax.axis_index("seq")
    tok, start, _ = token_rows(tok_ref[pl.ds(s, 1), :], lengths, None)
    position = tok - start + float(prefix)
    hid = hid_ref[...].astype(F32)
    scale = lax.rsqrt(jnp.mean(hid * hid, axis=-1, keepdims=True) + EPSILON)
    normed = (hid * scale * gain_ref[...]).astype(BF)

    angles = to_columns([position], n)[:, 0:1] * frow_ref[...]
    lane = lax.broadcasted_iota(jnp.int32, (n, 2 * ROPE), 1)
    first = lax.rem(lane, ROPE) < half
    cos = jnp.cos(angles)
    sin = jnp.sin(angles)
    query = dot(normed, wq_ref[...]).astype(BF)
    width = NOPE + ROPE
    pe = jnp.concatenate([query[:, NOPE:width], query[:, width + NOPE : 2 * width]], axis=1).astype(F32)
    partner = jnp.where(first, -pltpu.roll(pe, 2 * ROPE - half, 1), pltpu.roll(pe, half, 1))
    pe = (pe * cos + partner * sin).astype(BF)
    for i in range(q_ref.shape[0]):
        q_ref[i, :, 0:NOPE] = query[:, 0:NOPE]
        q_ref[i, :, NOPE : 2 * NOPE] = query[:, width : width + NOPE]
        q_ref[i, :, 2 * NOPE :] = pe

    raw = dot(wl_ref[...], normed, NT)
    lat = raw[:LATENT]
    lscale = lax.rsqrt(jnp.mean(lat * lat, axis=0, keepdims=True) + EPSILON)
    for i in range(0, LATENT, n):
        gain = jnp.broadcast_to(kvg_ref[:, i : i + n], (n, n)).T
        lat_ref[i : i + n, :] = (lat[i : i + n] * lscale * gain).astype(BF)
    angles = fcol_ref[...] * position
    cos = jnp.cos(angles)
    sin = jnp.sin(angles)
    top, low = raw[LATENT : LATENT + half], raw[LATENT + half :]
    lat_ref[LATENT : LATENT + half, :] = (top * cos - low * sin).astype(BF)
    lat_ref[LATENT + half :, :] = (low * cos + top * sin).astype(BF)


def attend_kernel(
    lengths, group, table, tok_ref, q_ref, pa_ref, pb_ref, la_ref, lb_ref, ku_ref, vu_ref,
    out_ref, s_ref, qf_ref, owner,
):
    j = pl.program_id(0)
    n = q_ref.shape[1]
    x, z, y, c = my_place()

    @pl.when(j == 0)
    def _():
        for g in range(table.shape[0]):
            for i in range(table.shape[1]):
                owner[table[g, i]] = g

    me = seq_id(x, lax.div(j, NY), lax.rem(j, NY), c)
    tok, start, grp = token_rows(tok_ref[pl.ds(me, 1), :], lengths, group)
    cols = to_columns([tok, start, grp], n)
    two = jnp.concatenate([cols, cols], axis=0)
    pos_q, start_q, grp_q = two[:, 0:1], two[:, 1:2], two[:, 2:3]

    for h in range(2):
        up = ku_ref[:, h * NOPE : (h + 1) * NOPE]
        nope = q_ref[0, :, h * NOPE : (h + 1) * NOPE]
        qf_ref[h * n : (h + 1) * n, :LATENT] = dot(nope, up, NT).astype(BF)
        qf_ref[h * n : (h + 1) * n, LATENT:] = q_ref[0, :, 2 * NOPE + h * ROPE : 2 * NOPE + (h + 1) * ROPE]
    qf = qf_ref[...]
    keys = (pa_ref, pb_ref, la_ref, lb_ref)
    high = jnp.full((2 * n, 1), MASKED, F32)
    for b, k_ref in enumerate(keys):
        sc = dot(qf, k_ref[...])
        for i in range(NX):
            holder = seq_id(x + i, z, y, c + b % 2)
            part = sc[:, i * n : (i + 1) * n]
            if b < 2:
                part = part + jnp.where(grp_q == owner[holder].astype(F32), 0.0, MASKED)
            else:
                pos_k = tok_ref[pl.ds(holder, 1), :].astype(F32)
                seen = jnp.logical_and(pos_k >= start_q, pos_k <= pos_q)
                part = jnp.where(seen, part, MASKED)
            s_ref[:, (b * NX + i) * n : (b * NX + i + 1) * n] = part
            high = jnp.maximum(high, jnp.max(part, axis=-1, keepdims=True))
    scale = (NOPE + ROPE) ** (-0.5)
    log2e = 1.4426950408889634
    top = jnp.where(high > 0.5 * MASKED, high, 0.0)
    den = jnp.zeros((2 * n, 1), F32)
    acc = jnp.zeros((2 * n, LATENT), F32)
    width = NX * n
    for b, k_ref in enumerate(keys):
        w = jnp.exp2((s_ref[:, b * width : (b + 1) * width] - top) * (scale * log2e))
        den = den + jnp.sum(w, axis=-1, keepdims=True)
        acc = acc + dot(w.astype(BF), k_ref[:LATENT, :], NT)
    some = den > 0.0
    att = (acc / jnp.where(some, den, 1.0)).astype(BF)
    lse = jnp.where(some, top * scale + jnp.log(jnp.where(some, den, 1.0)), MASKED)
    hi = lse.astype(BF).astype(F32)
    mid = (lse - hi).astype(BF).astype(F32)
    low = lse - hi - mid
    lane = lax.broadcasted_iota(jnp.int32, (n, 128), 1)
    stat = jnp.zeros((n, 128), F32)
    for h in range(2):
        rows = slice(h * n, (h + 1) * n)
        out_ref[0, :, h * VDIM : (h + 1) * VDIM] = dot(
            att[rows], vu_ref[:, h * VDIM : (h + 1) * VDIM]
        ).astype(BF)
        for i, term in enumerate((hi, mid, low)):
            stat = jnp.where(lane == 3 * h + i, term[rows], stat)
    out_ref[0, :, 2 * VDIM :] = stat.astype(BF)


def merge_kernel(got_ref, out_ref):
    m = got_ref.shape[0]
    for h in range(2):
        lse = []
        for i in range(m):
            st = got_ref[i, :, 2 * VDIM :].astype(F32)
            lse.append(st[:, 3 * h : 3 * h + 1] + st[:, 3 * h + 1 : 3 * h + 2] + st[:, 3 * h + 2 : 3 * h + 3])
        top = functools.reduce(jnp.maximum, lse)
        den = jnp.zeros_like(top)
        acc = jnp.zeros((got_ref.shape[1], VDIM), F32)
        for i in range(m):
            w = jnp.exp(lse[i] - top)
            den = den + w
            acc = acc + w * got_ref[i, :, h * VDIM : (h + 1) * VDIM].astype(F32)
        out_ref[:, h * VDIM : (h + 1) * VDIM] = (acc / den).astype(BF)


def finish_kernel(mix_ref, a_ref, b_ref, c_ref, d_ref, out_ref):
    total = a_ref[...].astype(F32) + b_ref[...].astype(F32) + c_ref[...].astype(F32) + d_ref[...].astype(F32)
    out_ref[...] = (mix_ref[...].astype(F32) + total).astype(BF)


def slots_kernel(ids_ref, gates_ref, oh_ref, hi_ref, lo_ref):
    experts = oh_ref.shape[0] // SLOTS
    n = oh_ref.shape[1]
    which = lax.broadcasted_iota(jnp.int32, (experts, n), 0)
    named = jnp.zeros((experts, n), F32)
    gate = jnp.zeros((experts, n), F32)
    for k in range(ids_ref.shape[0]):
        hit = which == ids_ref[k : k + 1, :]
        named = jnp.where(hit, 1.0, named)
        gate = jnp.where(hit, gates_ref[k : k + 1, :], gate)
    before = lax.broadcasted_iota(jnp.int32, (n, n), 0) < lax.broadcasted_iota(jnp.int32, (n, n), 1)
    count = dot(named.astype(BF), jnp.where(before, 1.0, 0.0).astype(BF))
    slot = jnp.where(named > 0.0, count, -1.0)
    ghi = gate.astype(BF).astype(F32)
    glo = gate - ghi
    level = lax.broadcasted_iota(jnp.int32, (SLOTS, n), 0).astype(F32)
    for e in range(experts):
        hit = slot[e : e + 1, :] == level
        rows = slice(e * SLOTS, (e + 1) * SLOTS)
        oh_ref[rows, :] = jnp.where(hit, 1.0, 0.0).astype(BF)
        hi_ref[rows, :] = jnp.where(hit, ghi[e : e + 1, :], 0.0).astype(BF)
        lo_ref[rows, :] = jnp.where(hit, glo[e : e + 1, :], 0.0).astype(BF)


def dispatch_kernel(v0, v1, v2, v3, hid_ref, wo_ref, wa_ref, wb_ref, gain_ref, oh_ref, out_ref, mix_ref, in_ref, acc_ref):
    d = hid_ref.shape[1]
    w = wa_ref.shape[2]
    q = mix_ref.shape[1]
    x, _, _, c = my_place()
    t = lax.axis_index("tensor")

    @pl.when(pl.program_id(0) == 0)
    def _():
        first = v0[...]
        others = (v1[...], v2[...], v3[...])
        for i in range(NX):
            for b, ref in enumerate((wa_ref, wb_ref)):
                col = pl.multiple_of((lax.rem(x + i, NX) * NC + lax.rem(c + b, NC)) * w, w)
                total = dot(first, wo_ref[:, pl.ds(col, w)])
                for j, v in enumerate(others):
                    total = total + dot(v, ref[i * len(others) + j])
                acc_ref[:, pl.ds(col, w)] = (hid_ref[:, pl.ds(col, w)].astype(F32) + total).astype(BF)
        mix_ref[...] = acc_ref[:, pl.ds(pl.multiple_of(t * q, q), q)]
        mixed = acc_ref[...].astype(F32)
        scale = lax.rsqrt(jnp.sum(mixed * mixed, axis=-1, keepdims=True) / d + EPSILON)
        in_ref[...] = (mixed * scale * gain_ref[...]).astype(BF)

    out_ref[...] = dot(oh_ref[...], in_ref[...]).astype(BF)


def expert_kernel(x_ref, wgu_ref, wd_ref, out_ref):
    hid = wd_ref.shape[0]
    wide = wgu_ref.shape[1] // 2
    both = dot(x_ref[...], wgu_ref[...])
    gate, up = both[:, :wide], both[:, wide:]
    act = (gate / (1.0 + jnp.exp(-gate)) * up).astype(BF)[:, :hid]
    out_ref[...] = dot(act, wd_ref[...]).astype(BF)


def combine_kernel(place, rows_ref, hi_ref, lo_ref, out_ref):
    tn = (((0,), (0,)), ((), ()))
    out_ref[...] = (dot(hi_ref[...], rows_ref[...], tn) + dot(lo_ref[...], rows_ref[...], tn)).astype(BF)


def whole(n):
    return [pl.BlockSpec(memory_space=VM)] * n


def local(
    hidden, attn_gain, w_query, w_latent_down, kv_gain, w_key_up, w_value_up, w_out, ffn_gain,
    w_gate_exp, w_up_exp, w_down_exp, page_pool, page_table, request_group, suffix_lengths,
    token_order, expert_ids, expert_gates,
):
    seq_count = lax.axis_size("seq")
    tensor_count = lax.axis_size("tensor")
    tensor_index = lax.axis_index("tensor")
    n, d = hidden.shape
    quarter = d // tensor_count
    prefix = page_table.shape[1] * page_pool.shape[1]
    tok = token_order.reshape(seq_count, n)
    params = pltpu.CompilerParams(vmem_limit_bytes=56 << 20)

    m = NZ * NY

    def spread(piece):
        got = [lax.ppermute(piece, "seq", seq_perm(i, 0, 0, 0)) for i in range(1, NX)]
        own = jnp.concatenate([piece] + got, axis=1)
        return own, lax.ppermute(own, "seq", seq_perm(0, 0, 0, 1))

    pages_a, pages_b = spread(page_pool[0].T)

    freq = ROPE_BASE ** (-2.0 * np.arange(ROPE // 2, dtype=np.float64) / ROPE)
    query, latent = pl.pallas_call(
        functools.partial(project_kernel, prefix),
        out_shape=(
            jax.ShapeDtypeStruct((m, n, w_query.shape[1]), BF),
            jax.ShapeDtypeStruct((KEY, n), BF),
        ),
        in_specs=[pl.BlockSpec(memory_space=SM)] + whole(8),
        out_specs=tuple(whole(2)),
        compiler_params=params,
        name="project",
    )(
        suffix_lengths, tok, jnp.asarray(freq[:, None], F32), jnp.asarray(np.tile(freq, 4)[None, :], F32), hidden,
        attn_gain.reshape(1, d), w_query, w_latent_down.T, kv_gain.reshape(1, LATENT),
    )

    lat_a, lat_b = spread(latent)
    queries = lax.all_to_all(query, "seq", 0, 0, tiled=True, axis_index_groups=zy_groups())

    x, _, _, c = my_place()
    share = d // (NX * NC)
    mine = lax.dynamic_slice_in_dim(w_out, (x * NC + c) * share, share, 1)
    other = jnp.stack([lax.ppermute(mine, "tensor", tensor_from(j, tensor_count)) for j in range(1, tensor_count)])
    wide = [other] + [lax.ppermute(other, "seq", seq_perm(i, 0, 0, 0)) for i in range(1, NX)]

    oh, ghi, glo = pl.pallas_call(
        slots_kernel,
        out_shape=(jax.ShapeDtypeStruct((seq_count * SLOTS, n), BF),) * 3,
        in_specs=whole(2),
        out_specs=tuple(whole(3)),
        compiler_params=params,
        name="slots",
    )(expert_ids.T, expert_gates.T)

    keys = NX * n

    def fixed(shape):
        return pl.BlockSpec(shape, lambda j, *_: (0,) * len(shape))

    partial = pl.pallas_call(
        attend_kernel,
        out_shape=jax.ShapeDtypeStruct((m, n, 3 * VDIM), BF),
        grid_spec=pltpu.PrefetchScalarGridSpec(
            num_scalar_prefetch=3,
            grid=(m,),
            in_specs=[fixed(tok.shape)]
            + [pl.BlockSpec((1,) + query.shape[1:], lambda j, *_: (j, 0, 0))]
            + [fixed((KEY, keys))] * 4
            + [fixed(w_key_up.shape), fixed(w_value_up.shape)],
            out_specs=pl.BlockSpec((1, n, 3 * VDIM), lambda j, *_: (j, 0, 0)),
            scratch_shapes=[
                pltpu.VMEM((2 * n, 4 * keys), F32),
                pltpu.VMEM((2 * n, KEY), BF),
                pltpu.SMEM((seq_count,), jnp.int32),
            ],
        ),
        compiler_params=params,
        name="attend",
    )(
        suffix_lengths, request_group, page_table, tok, queries, pages_a, pages_b, lat_a, lat_b, w_key_up, w_value_up
    )

    got = lax.all_to_all(partial, "seq", 0, 0, tiled=True, axis_index_groups=zy_groups())
    values = pl.pallas_call(
        merge_kernel,
        out_shape=jax.ShapeDtypeStruct((n, 2 * VDIM), BF),
        in_specs=whole(1),
        out_specs=whole(1)[0],
        compiler_params=params,
        name="merge",
    )(got)
    all_values = [values] + [
        lax.ppermute(values, "tensor", tensor_from(j, tensor_count)) for j in range(1, tensor_count)
    ]
    wide, _ = lax.optimization_barrier((wide, values))
    wide = jnp.concatenate(wide, axis=0)
    wide_b = lax.ppermute(wide, "seq", seq_perm(0, 0, 0, 1))

    piece = jax.ShapeDtypeStruct((n, quarter), BF)
    rows = seq_count * SLOTS
    block = rows // 4
    outbound, mixed = pl.pallas_call(
        dispatch_kernel,
        out_shape=(jax.ShapeDtypeStruct((rows, d), BF), piece),
        grid=(rows // block,),
        in_specs=[fixed(values.shape)] * 4
        + [fixed(hidden.shape), fixed(w_out.shape), fixed(wide.shape), fixed(wide.shape), fixed((1, d))]
        + [pl.BlockSpec((block, n), lambda i: (i, 0))],
        out_specs=(pl.BlockSpec((block, d), lambda i: (i, 0)), fixed((n, quarter))),
        scratch_shapes=[pltpu.VMEM((n, d), BF), pltpu.VMEM((n, d), BF)],
        compiler_params=params,
        name="dispatch",
    )(*all_values, hidden, w_out, wide, wide_b, ffn_gain.reshape(1, d), oh)
    arrived = lax.all_to_all(outbound.reshape(seq_count, SLOTS, d), "seq", 0, 0, tiled=True)
    hid = w_gate_exp.shape[2]
    fill = jnp.zeros((d, -hid % 128), BF)
    both = jnp.concatenate([w_gate_exp[0], fill, w_up_exp[0], fill], axis=1)
    results = pl.pallas_call(
        expert_kernel,
        out_shape=jax.ShapeDtypeStruct((rows, d), BF),
        grid=(rows // block,),
        in_specs=[pl.BlockSpec((block, d), lambda i: (i, 0)), fixed(both.shape), fixed((hid, d))],
        out_specs=pl.BlockSpec((block, d), lambda i: (i, 0)),
        compiler_params=params,
        name="expert",
    )(arrived.reshape(rows, d), both, w_down_exp[0])
    back = lax.all_to_all(results.reshape(seq_count, SLOTS, d), "seq", 0, 0, tiled=True)
    place = tensor_index.astype(jnp.int32).reshape(1)

    def combined(i):
        return pl.pallas_call(
            combine_kernel,
            out_shape=piece,
            grid_spec=pltpu.PrefetchScalarGridSpec(
                num_scalar_prefetch=1,
                grid=(1,),
                in_specs=[
                    pl.BlockSpec((rows, quarter), lambda j, place: (0, lax.rem(place[0] + i, tensor_count))),
                    fixed(ghi.shape),
                    fixed(glo.shape),
                ],
                out_specs=fixed((n, quarter)),
            ),
            compiler_params=params,
            name="combine",
        )(place, back.reshape(rows, d), ghi, glo)

    sums = [None] * tensor_count
    for i in (2, 1, 3):
        sums[i] = lax.ppermute(combined(i), "tensor", tensor_from(-i, tensor_count))
    sums[0] = combined(0)
    hidden_out = pl.pallas_call(
        finish_kernel, out_shape=piece, in_specs=whole(5), out_specs=whole(1)[0], compiler_params=params, name="finish"
    )(mixed, *sums)
    width = KEY // tensor_count
    cache_part = lax.dynamic_slice_in_dim(latent, tensor_index * width, width, 0).T
    return (hidden_out, cache_part)


def solution(mesh):
    placed = (
        P("seq", None),
        P(),
        P(None, "tensor"),
        P(),
        P(),
        P(None, "tensor"),
        P(None, "tensor"),
        P("tensor", None),
        P(),
        P("seq", None, "tensor"),
        P("seq", None, "tensor"),
        P("seq", "tensor", None),
        P("seq", None, None),
        P(),
        P(),
        P(),
        P(),
        P("seq", None),
        P("seq", None),
    )

    return jax.shard_map(
        local,
        mesh=mesh,
        in_specs=placed,
        out_specs=(P("seq", "tensor"), P("seq", "tensor")),
        check_vma=False,
    )
```

```python
import functools

import jax
import jax.numpy as jnp
import numpy as np
from jax import lax
from jax.experimental import pallas as pl
from jax.experimental.pallas import tpu as pltpu
from jax.sharding import PartitionSpec as P


NOPE = 128
ROPE = 64
VDIM = 128
LATENT = 512
KEY = LATENT + ROPE
SLOTS = 16
STATS = 16
EPSILON = 1e-06
ROPE_BASE = 50000.0
MASKED = -1e30

NX, NZ, NY, NC = 4, 2, 4, 2
BF = jnp.bfloat16
F32 = jnp.float32
NT = (((1,), (1,)), ((), ()))
VM = pltpu.MemorySpace.VMEM
SM = pltpu.MemorySpace.SMEM


def seq_id(x, z, y, c):
    return (((x % NX) * NZ + z % NZ) * NY + y % NY) * NC + c % NC


def seq_perm(dx, dz, dy, dc):
    pairs = []
    for x in range(NX):
        for z in range(NZ):
            for y in range(NY):
                for c in range(NC):
                    pairs.append((seq_id(x + dx, z + dz, y + dy, c + dc), seq_id(x, z, y, c)))
    return pairs


def tensor_from(d, n):
    return [((t + d) % n, t) for t in range(n)]


def zy_groups():
    return [
        [seq_id(x, z, y, c) for z in range(NZ) for y in range(NY)]
        for x in range(NX)
        for c in range(NC)
    ]


def my_place():
    s = lax.axis_index("seq")
    c = lax.rem(s, NC)
    y = lax.rem(lax.div(s, NC), NY)
    z = lax.rem(lax.div(s, NC * NY), NZ)
    x = lax.div(s, NC * NY * NZ)
    return x, z, y, c


def dot(a, b, dims=(((1,), (0,)), ((), ()))):
    return lax.dot_general(a, b, dims, preferred_element_type=F32)


def token_rows(tok, lengths, group):
    tok = tok.astype(F32)
    start = jnp.zeros_like(tok)
    grp = jnp.zeros_like(tok)
    end = jnp.int32(0)
    for r in range(lengths.shape[0]):
        begin = end
        end = end + lengths[r]
        ef = end.astype(F32)
        bf = begin.astype(F32)
        past = tok >= ef
        start = jnp.where(past, ef, start)
        if group is not None:
            inside = jnp.logical_and(tok >= bf, tok < ef)
            grp = jnp.where(inside, group[r].astype(F32), grp)
    return tok, start, grp


def to_columns(rows, n):
    which = lax.broadcasted_iota(jnp.int32, (n, n), 0)
    out = jnp.zeros((n, n), F32)
    for i, row in enumerate(rows):
        out = jnp.where(which == i, jnp.broadcast_to(row, (n, n)), out)
    return out.T


def project_kernel(prefix, lengths, tok_ref, fcol_ref, frow_ref, hid_ref, gain_ref, wq_ref, wl_ref, kvg_ref, q_ref, lat_ref):
    n = hid_ref.shape[0]
    half = ROPE // 2
    s = lax.axis_index("seq")
    tok, start, _ = token_rows(tok_ref[pl.ds(s, 1), :], lengths, None)
    position = tok - start + float(prefix)
    hid = hid_ref[...].astype(F32)
    scale = lax.rsqrt(jnp.mean(hid * hid, axis=-1, keepdims=True) + EPSILON)
    normed = (hid * scale * gain_ref[...]).astype(BF)

    angles = to_columns([position], n)[:, 0:1] * frow_ref[...]
    lane = lax.broadcasted_iota(jnp.int32, (n, 2 * ROPE), 1)
    first = lax.rem(lane, ROPE) < half
    cos = jnp.cos(angles)
    sin = jnp.sin(angles)
    query = dot(normed, wq_ref[...]).astype(BF)
    width = NOPE + ROPE
    pe = jnp.concatenate([query[:, NOPE:width], query[:, width + NOPE : 2 * width]], axis=1).astype(F32)
    partner = jnp.where(first, -pltpu.roll(pe, 2 * ROPE - half, 1), pltpu.roll(pe, half, 1))
    pe = (pe * cos + partner * sin).astype(BF)
    for i in range(q_ref.shape[0]):
        q_ref[i, :, 0:NOPE] = query[:, 0:NOPE]
        q_ref[i, :, NOPE : 2 * NOPE] = query[:, width : width + NOPE]
        q_ref[i, :, 2 * NOPE :] = pe

    raw = dot(wl_ref[...], normed, NT)
    lat = raw[:LATENT]
    lscale = lax.rsqrt(jnp.mean(lat * lat, axis=0, keepdims=True) + EPSILON)
    for i in range(0, LATENT, n):
        gain = jnp.broadcast_to(kvg_ref[:, i : i + n], (n, n)).T
        lat_ref[i : i + n, :] = (lat[i : i + n] * lscale * gain).astype(BF)
    angles = fcol_ref[...] * position
    cos = jnp.cos(angles)
    sin = jnp.sin(angles)
    top, low = raw[LATENT : LATENT + half], raw[LATENT + half :]
    lat_ref[LATENT : LATENT + half, :] = (top * cos - low * sin).astype(BF)
    lat_ref[LATENT + half :, :] = (low * cos + top * sin).astype(BF)


def attend_kernel(
    lengths, group, table, tok_ref, q_ref, pa_ref, pb_ref, la_ref, lb_ref, ku_ref, vu_ref,
    out_ref, s_ref, qf_ref, owner,
):
    j = pl.program_id(0)
    n = q_ref.shape[1]
    x, z, y, c = my_place()

    @pl.when(j == 0)
    def _():
        for g in range(table.shape[0]):
            for i in range(table.shape[1]):
                owner[table[g, i]] = g

    me = seq_id(x, lax.div(j, NY), lax.rem(j, NY), c)
    tok, start, grp = token_rows(tok_ref[pl.ds(me, 1), :], lengths, group)
    cols = to_columns([tok, start, grp], n)
    two = jnp.concatenate([cols, cols], axis=0)
    pos_q, start_q, grp_q = two[:, 0:1], two[:, 1:2], two[:, 2:3]

    for h in range(2):
        up = ku_ref[:, h * NOPE : (h + 1) * NOPE]
        nope = q_ref[0, :, h * NOPE : (h + 1) * NOPE]
        qf_ref[h * n : (h + 1) * n, :LATENT] = dot(nope, up, NT).astype(BF)
        qf_ref[h * n : (h + 1) * n, LATENT:] = q_ref[0, :, 2 * NOPE + h * ROPE : 2 * NOPE + (h + 1) * ROPE]
    qf = qf_ref[...]
    keys = (pa_ref, pb_ref, la_ref, lb_ref)
    high = jnp.full((2 * n, 1), MASKED, F32)
    for b, k_ref in enumerate(keys):
        sc = dot(qf, k_ref[...])
        for i in range(NX):
            holder = seq_id(x + i, z, y, c + b % 2)
            part = sc[:, i * n : (i + 1) * n]
            if b < 2:
                part = part + jnp.where(grp_q == owner[holder].astype(F32), 0.0, MASKED)
            else:
                pos_k = tok_ref[pl.ds(holder, 1), :].astype(F32)
                seen = jnp.logical_and(pos_k >= start_q, pos_k <= pos_q)
                part = jnp.where(seen, part, MASKED)
            s_ref[:, (b * NX + i) * n : (b * NX + i + 1) * n] = part
            high = jnp.maximum(high, jnp.max(part, axis=-1, keepdims=True))
    scale = (NOPE + ROPE) ** (-0.5)
    log2e = 1.4426950408889634
    top = jnp.where(high > 0.5 * MASKED, high, 0.0)
    den = jnp.zeros((2 * n, 1), F32)
    acc = jnp.zeros((2 * n, LATENT), F32)
    width = NX * n
    for b, k_ref in enumerate(keys):
        w = jnp.exp2((s_ref[:, b * width : (b + 1) * width] - top) * (scale * log2e))
        den = den + jnp.sum(w, axis=-1, keepdims=True)
        acc = acc + dot(w.astype(BF), k_ref[:LATENT, :], NT)
    some = den > 0.0
    att = (acc / jnp.where(some, den, 1.0)).astype(BF)
    lse = jnp.where(some, top * scale + jnp.log(jnp.where(some, den, 1.0)), MASKED)
    hi = lse.astype(BF).astype(F32)
    mid = (lse - hi).astype(BF).astype(F32)
    low = lse - hi - mid
    lane = lax.broadcasted_iota(jnp.int32, (n, 128), 1)
    stat = jnp.zeros((n, 128), F32)
    for h in range(2):
        rows = slice(h * n, (h + 1) * n)
        out_ref[0, :n, h * VDIM : (h + 1) * VDIM] = dot(
            att[rows], vu_ref[:, h * VDIM : (h + 1) * VDIM]
        ).astype(BF)
        for i, term in enumerate((hi, mid, low)):
            stat = jnp.where(lane == 3 * h + i, term[rows], stat)
    out_ref[0, n:, :VDIM] = stat.T[:STATS].astype(BF)
    out_ref[0, n:, VDIM:] = jnp.zeros((STATS, VDIM), BF)


def merge_kernel(got_ref, out_ref):
    m = got_ref.shape[0]
    n = out_ref.shape[0]
    stats = jnp.concatenate([got_ref[i, n:, :VDIM] for i in range(m)], axis=0).astype(F32).T
    for h in range(2):
        lse = []
        for i in range(m):
            at = i * STATS + 3 * h
            lse.append(stats[:, at : at + 1] + stats[:, at + 1 : at + 2] + stats[:, at + 2 : at + 3])
        top = functools.reduce(jnp.maximum, lse)
        den = jnp.zeros_like(top)
        acc = jnp.zeros((n, VDIM), F32)
        for i in range(m):
            w = jnp.exp(lse[i] - top)
            den = den + w
            acc = acc + w * got_ref[i, :n, h * VDIM : (h + 1) * VDIM].astype(F32)
        out_ref[:, h * VDIM : (h + 1) * VDIM] = (acc / den).astype(BF)


def finish_kernel(mix_ref, a_ref, b_ref, c_ref, d_ref, out_ref):
    total = a_ref[...].astype(F32) + b_ref[...].astype(F32) + c_ref[...].astype(F32) + d_ref[...].astype(F32)
    out_ref[...] = (mix_ref[...].astype(F32) + total).astype(BF)


def slots_kernel(ids_ref, gates_ref, oh_ref, hi_ref, lo_ref):
    experts = oh_ref.shape[0] // SLOTS
    n = oh_ref.shape[1]
    which = lax.broadcasted_iota(jnp.int32, (experts, n), 0)
    named = jnp.zeros((experts, n), F32)
    gate = jnp.zeros((experts, n), F32)
    for k in range(ids_ref.shape[0]):
        hit = which == ids_ref[k : k + 1, :]
        named = jnp.where(hit, 1.0, named)
        gate = jnp.where(hit, gates_ref[k : k + 1, :], gate)
    before = lax.broadcasted_iota(jnp.int32, (n, n), 0) < lax.broadcasted_iota(jnp.int32, (n, n), 1)
    count = dot(named.astype(BF), jnp.where(before, 1.0, 0.0).astype(BF))
    slot = jnp.where(named > 0.0, count, -1.0)
    ghi = gate.astype(BF).astype(F32)
    glo = gate - ghi
    level = lax.broadcasted_iota(jnp.int32, (SLOTS, n), 0).astype(F32)
    per = n // SLOTS
    for first in range(0, experts, per):
        parts = ([], [])
        for e in range(first, first + per):
            hit = slot[e : e + 1, :] == level
            oh_ref[e * SLOTS : (e + 1) * SLOTS, :] = jnp.where(hit, 1.0, 0.0).astype(BF)
            for part, v in zip(parts, (ghi, glo)):
                part.append(jnp.where(hit, v[e : e + 1, :], 0.0))
        for ref, part in zip((hi_ref, lo_ref), parts):
            ref[:, first * SLOTS : (first + per) * SLOTS] = jnp.concatenate(part, axis=0).T.astype(BF)


def dispatch_kernel(v0, v1, v2, v3, hid_ref, wo_ref, wa_ref, wb_ref, gain_ref, oh_ref, out_ref, mix_ref, in_ref, acc_ref):
    d = hid_ref.shape[1]
    w = wa_ref.shape[2]
    q = mix_ref.shape[1]
    x, _, _, c = my_place()
    t = lax.axis_index("tensor")

    @pl.when(pl.program_id(0) == 0)
    def _():
        first = v0[...]
        others = (v1[...], v2[...], v3[...])
        for i in range(NX):
            for b, ref in enumerate((wa_ref, wb_ref)):
                col = pl.multiple_of((lax.rem(x + i, NX) * NC + lax.rem(c + b, NC)) * w, w)
                total = dot(first, wo_ref[:, pl.ds(col, w)])
                for j, v in enumerate(others):
                    total = total + dot(v, ref[i * len(others) + j])
                acc_ref[:, pl.ds(col, w)] = (hid_ref[:, pl.ds(col, w)].astype(F32) + total).astype(BF)
        mix_ref[...] = acc_ref[:, pl.ds(pl.multiple_of(t * q, q), q)]
        mixed = acc_ref[...].astype(F32)
        scale = lax.rsqrt(jnp.sum(mixed * mixed, axis=-1, keepdims=True) / d + EPSILON)
        in_ref[...] = (mixed * scale * gain_ref[...]).astype(BF)

    out_ref[...] = dot(oh_ref[...], in_ref[...]).astype(BF)


def expert_kernel(x_ref, wgu_ref, wd_ref, out_ref):
    hid = wd_ref.shape[0]
    wide = wgu_ref.shape[1] // 2
    both = dot(x_ref[...], wgu_ref[...])
    gate, up = both[:, :wide], both[:, wide:]
    act = (gate / (1.0 + jnp.exp(-gate)) * up).astype(BF)[:, :hid]
    out_ref[...] = dot(act, wd_ref[...]).astype(BF)


def combine_kernel(place, rows_ref, hi_ref, lo_ref, out_ref):
    rows = rows_ref[...]
    out_ref[...] = (dot(hi_ref[...], rows) + dot(lo_ref[...], rows)).astype(BF)


def whole(n):
    return [pl.BlockSpec(memory_space=VM)] * n


def local(
    hidden, attn_gain, w_query, w_latent_down, kv_gain, w_key_up, w_value_up, w_out, ffn_gain,
    w_gate_exp, w_up_exp, w_down_exp, page_pool, page_table, request_group, suffix_lengths,
    token_order, expert_ids, expert_gates,
):
    seq_count = lax.axis_size("seq")
    tensor_count = lax.axis_size("tensor")
    tensor_index = lax.axis_index("tensor")
    n, d = hidden.shape
    quarter = d // tensor_count
    prefix = page_table.shape[1] * page_pool.shape[1]
    tok = token_order.reshape(seq_count, n)
    params = pltpu.CompilerParams(vmem_limit_bytes=28 << 20)

    m = NZ * NY

    def spread(piece):
        got = [lax.ppermute(piece, "seq", seq_perm(i, 0, 0, 0)) for i in range(1, NX)]
        own = jnp.concatenate([piece] + got, axis=1)
        return own, lax.ppermute(own, "seq", seq_perm(0, 0, 0, 1))

    pages_a, pages_b = spread(page_pool[0].T)

    freq = ROPE_BASE ** (-2.0 * np.arange(ROPE // 2, dtype=np.float64) / ROPE)
    query, latent = pl.pallas_call(
        functools.partial(project_kernel, prefix),
        out_shape=(
            jax.ShapeDtypeStruct((m, n, w_query.shape[1]), BF),
            jax.ShapeDtypeStruct((KEY, n), BF),
        ),
        in_specs=[pl.BlockSpec(memory_space=SM)] + whole(8),
        out_specs=tuple(whole(2)),
        compiler_params=params,
        name="project",
    )(
        suffix_lengths, tok, jnp.asarray(freq[:, None], F32), jnp.asarray(np.tile(freq, 4)[None, :], F32), hidden,
        attn_gain.reshape(1, d), w_query, w_latent_down.T, kv_gain.reshape(1, LATENT),
    )

    lat_a, lat_b = spread(latent)
    queries = lax.all_to_all(query, "seq", 0, 0, tiled=True, axis_index_groups=zy_groups())

    x, _, _, c = my_place()
    share = d // (NX * NC)
    mine = lax.dynamic_slice_in_dim(w_out, (x * NC + c) * share, share, 1)
    other = jnp.stack([lax.ppermute(mine, "tensor", tensor_from(j, tensor_count)) for j in range(1, tensor_count)])
    wide = [other] + [lax.ppermute(other, "seq", seq_perm(i, 0, 0, 0)) for i in range(1, NX)]

    oh, ghi, glo = pl.pallas_call(
        slots_kernel,
        out_shape=(jax.ShapeDtypeStruct((seq_count * SLOTS, n), BF),)
        + (jax.ShapeDtypeStruct((n, seq_count * SLOTS), BF),) * 2,
        in_specs=whole(2),
        out_specs=tuple(whole(3)),
        compiler_params=params,
        name="slots",
    )(expert_ids.T, expert_gates.T)

    keys = NX * n

    def fixed(shape):
        return pl.BlockSpec(shape, lambda j, *_: (0,) * len(shape))

    partial = pl.pallas_call(
        attend_kernel,
        out_shape=jax.ShapeDtypeStruct((m, n + STATS, 2 * VDIM), BF),
        grid_spec=pltpu.PrefetchScalarGridSpec(
            num_scalar_prefetch=3,
            grid=(m,),
            in_specs=[fixed(tok.shape)]
            + [pl.BlockSpec((1,) + query.shape[1:], lambda j, *_: (j, 0, 0))]
            + [fixed((KEY, keys))] * 4
            + [fixed(w_key_up.shape), fixed(w_value_up.shape)],
            out_specs=pl.BlockSpec((1, n + STATS, 2 * VDIM), lambda j, *_: (j, 0, 0)),
            scratch_shapes=[
                pltpu.VMEM((2 * n, 4 * keys), F32),
                pltpu.VMEM((2 * n, KEY), BF),
                pltpu.SMEM((seq_count,), jnp.int32),
            ],
        ),
        compiler_params=params,
        name="attend",
    )(
        suffix_lengths, request_group, page_table, tok, queries, pages_a, pages_b, lat_a, lat_b, w_key_up, w_value_up
    )

    got = lax.all_to_all(partial, "seq", 0, 0, tiled=True, axis_index_groups=zy_groups())
    values = pl.pallas_call(
        merge_kernel,
        out_shape=jax.ShapeDtypeStruct((n, 2 * VDIM), BF),
        in_specs=whole(1),
        out_specs=whole(1)[0],
        compiler_params=params,
        name="merge",
    )(got)
    all_values = [values] + [
        lax.ppermute(values, "tensor", tensor_from(j, tensor_count)) for j in range(1, tensor_count)
    ]
    wide, _ = lax.optimization_barrier((wide, values))
    wide = jnp.concatenate(wide, axis=0)
    wide_b = lax.ppermute(wide, "seq", seq_perm(0, 0, 0, 1))

    piece = jax.ShapeDtypeStruct((n, quarter), BF)
    rows = seq_count * SLOTS
    block = rows // 4
    outbound, mixed = pl.pallas_call(
        dispatch_kernel,
        out_shape=(jax.ShapeDtypeStruct((rows, d), BF), piece),
        grid=(rows // block,),
        in_specs=[fixed(values.shape)] * 4
        + [fixed(hidden.shape), fixed(w_out.shape), fixed(wide.shape), fixed(wide.shape), fixed((1, d))]
        + [pl.BlockSpec((block, n), lambda i: (i, 0))],
        out_specs=(pl.BlockSpec((block, d), lambda i: (i, 0)), fixed((n, quarter))),
        scratch_shapes=[pltpu.VMEM((n, d), BF), pltpu.VMEM((n, d), BF)],
        compiler_params=params,
        name="dispatch",
    )(*all_values, hidden, w_out, wide, wide_b, ffn_gain.reshape(1, d), oh)
    arrived = lax.all_to_all(outbound.reshape(seq_count, SLOTS, d), "seq", 0, 0, tiled=True)
    hid = w_gate_exp.shape[2]
    fill = jnp.zeros((d, -hid % 128), BF)
    both = jnp.concatenate([w_gate_exp[0], fill, w_up_exp[0], fill], axis=1)
    results = pl.pallas_call(
        expert_kernel,
        out_shape=jax.ShapeDtypeStruct((rows, d), BF),
        grid=(rows // block,),
        in_specs=[pl.BlockSpec((block, d), lambda i: (i, 0)), fixed(both.shape), fixed((hid, d))],
        out_specs=pl.BlockSpec((block, d), lambda i: (i, 0)),
        compiler_params=params,
        name="expert",
    )(arrived.reshape(rows, d), both, w_down_exp[0])
    back = lax.all_to_all(results.reshape(seq_count, SLOTS, d), "seq", 0, 0, tiled=True)
    place = tensor_index.astype(jnp.int32).reshape(1)

    def combined(i):
        return pl.pallas_call(
            combine_kernel,
            out_shape=piece,
            grid_spec=pltpu.PrefetchScalarGridSpec(
                num_scalar_prefetch=1,
                grid=(1,),
                in_specs=[
                    pl.BlockSpec((rows, quarter), lambda j, place: (0, lax.rem(place[0] + i, tensor_count))),
                    fixed(ghi.shape),
                    fixed(glo.shape),
                ],
                out_specs=fixed((n, quarter)),
            ),
            compiler_params=params,
            name="combine",
        )(place, back.reshape(rows, d), ghi, glo)

    sums = [None] * tensor_count
    for i in (2, 1, 3):
        sums[i] = lax.ppermute(combined(i), "tensor", tensor_from(-i, tensor_count))
    sums[0] = combined(0)
    hidden_out = pl.pallas_call(
        finish_kernel, out_shape=piece, in_specs=whole(5), out_specs=whole(1)[0], compiler_params=params, name="finish"
    )(mixed, *sums)
    width = KEY // tensor_count
    cache_part = lax.dynamic_slice_in_dim(latent, tensor_index * width, width, 0).T
    return (hidden_out, cache_part)


def solution(mesh):
    placed = (
        P("seq", None),
        P(),
        P(None, "tensor"),
        P(),
        P(),
        P(None, "tensor"),
        P(None, "tensor"),
        P("tensor", None),
        P(),
        P("seq", None, "tensor"),
        P("seq", None, "tensor"),
        P("seq", "tensor", None),
        P("seq", None, None),
        P(),
        P(),
        P(),
        P(),
        P("seq", None),
        P("seq", None),
    )

    return jax.shard_map(
        local,
        mesh=mesh,
        in_specs=placed,
        out_specs=(P("seq", "tensor"), P("seq", "tensor")),
        check_vma=False,
    )
```

```python
import functools

import jax
import jax.numpy as jnp
import numpy as np
from jax import lax
from jax.experimental import pallas as pl
from jax.experimental.pallas import tpu as pltpu
from jax.sharding import PartitionSpec as P


NOPE = 128
ROPE = 64
VDIM = 128
LATENT = 512
KEY = LATENT + ROPE
SLOTS = 16
STATS = 16
EPSILON = 1e-06
ROPE_BASE = 50000.0
MASKED = -1e30

NX, NZ, NY, NC = 4, 2, 4, 2
BF = jnp.bfloat16
F32 = jnp.float32
NT = (((1,), (1,)), ((), ()))
VM = pltpu.MemorySpace.VMEM
SM = pltpu.MemorySpace.SMEM


def seq_id(x, z, y, c):
    return (((x % NX) * NZ + z % NZ) * NY + y % NY) * NC + c % NC


def seq_perm(dx, dz, dy, dc):
    pairs = []
    for x in range(NX):
        for z in range(NZ):
            for y in range(NY):
                for c in range(NC):
                    pairs.append((seq_id(x + dx, z + dz, y + dy, c + dc), seq_id(x, z, y, c)))
    return pairs


def tensor_from(d, n):
    return [((t + d) % n, t) for t in range(n)]


def zy_groups():
    return [
        [seq_id(x, z, y, c) for z in range(NZ) for y in range(NY)]
        for x in range(NX)
        for c in range(NC)
    ]


def my_place():
    s = lax.axis_index("seq")
    c = lax.rem(s, NC)
    y = lax.rem(lax.div(s, NC), NY)
    z = lax.rem(lax.div(s, NC * NY), NZ)
    x = lax.div(s, NC * NY * NZ)
    return x, z, y, c


def dot(a, b, dims=(((1,), (0,)), ((), ()))):
    return lax.dot_general(a, b, dims, preferred_element_type=F32)


def token_rows(tok, lengths, group):
    tok = tok.astype(F32)
    start = jnp.zeros_like(tok)
    grp = jnp.zeros_like(tok)
    end = jnp.int32(0)
    for r in range(lengths.shape[0]):
        begin = end
        end = end + lengths[r]
        ef = end.astype(F32)
        bf = begin.astype(F32)
        past = tok >= ef
        start = jnp.where(past, ef, start)
        if group is not None:
            inside = jnp.logical_and(tok >= bf, tok < ef)
            grp = jnp.where(inside, group[r].astype(F32), grp)
    return tok, start, grp


def to_columns(rows, n):
    which = lax.broadcasted_iota(jnp.int32, (n, n), 0)
    out = jnp.zeros((n, n), F32)
    for i, row in enumerate(rows):
        out = jnp.where(which == i, jnp.broadcast_to(row, (n, n)), out)
    return out.T


def project_kernel(prefix, lengths, tok_ref, fcol_ref, frow_ref, hid_ref, gain_ref, wq_ref, wl_ref, kvg_ref, q_ref, lat_ref):
    n = hid_ref.shape[0]
    half = ROPE // 2
    s = lax.axis_index("seq")
    tok, start, _ = token_rows(tok_ref[pl.ds(s, 1), :], lengths, None)
    position = tok - start + float(prefix)
    hid = hid_ref[...].astype(F32)
    scale = lax.rsqrt(jnp.mean(hid * hid, axis=-1, keepdims=True) + EPSILON)
    normed = (hid * scale * gain_ref[...]).astype(BF)

    angles = to_columns([position], n)[:, 0:1] * frow_ref[...]
    lane = lax.broadcasted_iota(jnp.int32, (n, 2 * ROPE), 1)
    first = lax.rem(lane, ROPE) < half
    cos = jnp.cos(angles)
    sin = jnp.sin(angles)
    query = dot(normed, wq_ref[...]).astype(BF)
    width = NOPE + ROPE
    pe = jnp.concatenate([query[:, NOPE:width], query[:, width + NOPE : 2 * width]], axis=1).astype(F32)
    partner = jnp.where(first, -pltpu.roll(pe, 2 * ROPE - half, 1), pltpu.roll(pe, half, 1))
    pe = (pe * cos + partner * sin).astype(BF)
    for i in range(q_ref.shape[0]):
        q_ref[i, :, 0:NOPE] = query[:, 0:NOPE]
        q_ref[i, :, NOPE : 2 * NOPE] = query[:, width : width + NOPE]
        q_ref[i, :, 2 * NOPE :] = pe

    raw = dot(wl_ref[...], normed, NT)
    lat = raw[:LATENT]
    lscale = lax.rsqrt(jnp.mean(lat * lat, axis=0, keepdims=True) + EPSILON)
    for i in range(0, LATENT, n):
        gain = jnp.broadcast_to(kvg_ref[:, i : i + n], (n, n)).T
        lat_ref[i : i + n, :] = (lat[i : i + n] * lscale * gain).astype(BF)
    angles = fcol_ref[...] * position
    cos = jnp.cos(angles)
    sin = jnp.sin(angles)
    top, low = raw[LATENT : LATENT + half], raw[LATENT + half :]
    lat_ref[LATENT : LATENT + half, :] = (top * cos - low * sin).astype(BF)
    lat_ref[LATENT + half :, :] = (low * cos + top * sin).astype(BF)


def attend_kernel(
    lengths, group, table, tok_ref, q_ref, pa_ref, pb_ref, la_ref, lb_ref, ku_ref, vu_ref,
    out_ref, s_ref, qf_ref, owner,
):
    j = pl.program_id(0)
    n = q_ref.shape[1]
    x, z, y, c = my_place()

    @pl.when(j == 0)
    def _():
        for g in range(table.shape[0]):
            for i in range(table.shape[1]):
                owner[table[g, i]] = g

    me = seq_id(x, lax.div(j, NY), lax.rem(j, NY), c)
    tok, start, grp = token_rows(tok_ref[pl.ds(me, 1), :], lengths, group)
    cols = to_columns([tok, start, grp], n)
    two = jnp.concatenate([cols, cols], axis=0)
    pos_q, start_q, grp_q = two[:, 0:1], two[:, 1:2], two[:, 2:3]

    for h in range(2):
        up = ku_ref[:, h * NOPE : (h + 1) * NOPE]
        nope = q_ref[0, :, h * NOPE : (h + 1) * NOPE]
        qf_ref[h * n : (h + 1) * n, :LATENT] = dot(nope, up, NT).astype(BF)
        qf_ref[h * n : (h + 1) * n, LATENT:] = q_ref[0, :, 2 * NOPE + h * ROPE : 2 * NOPE + (h + 1) * ROPE]
    qf = qf_ref[...]
    keys = (pa_ref, pb_ref, la_ref, lb_ref)
    high = jnp.full((2 * n, 1), MASKED, F32)
    for b, k_ref in enumerate(keys):
        sc = dot(qf, k_ref[...])
        for i in range(NX):
            holder = seq_id(x + i, z, y, c + b % 2)
            part = sc[:, i * n : (i + 1) * n]
            if b < 2:
                part = part + jnp.where(grp_q == owner[holder].astype(F32), 0.0, MASKED)
            else:
                pos_k = tok_ref[pl.ds(holder, 1), :].astype(F32)
                seen = jnp.logical_and(pos_k >= start_q, pos_k <= pos_q)
                part = jnp.where(seen, part, MASKED)
            s_ref[:, (b * NX + i) * n : (b * NX + i + 1) * n] = part
            high = jnp.maximum(high, jnp.max(part, axis=-1, keepdims=True))
    scale = (NOPE + ROPE) ** (-0.5)
    log2e = 1.4426950408889634
    top = jnp.where(high > 0.5 * MASKED, high, 0.0)
    den = jnp.zeros((2 * n, 1), F32)
    acc = jnp.zeros((2 * n, LATENT), F32)
    width = NX * n
    for b, k_ref in enumerate(keys):
        w = jnp.exp2((s_ref[:, b * width : (b + 1) * width] - top) * (scale * log2e))
        den = den + jnp.sum(w, axis=-1, keepdims=True)
        acc = acc + dot(w.astype(BF), k_ref[:LATENT, :], NT)
    some = den > 0.0
    att = (acc / jnp.where(some, den, 1.0)).astype(BF)
    lse = jnp.where(some, top * scale + jnp.log(jnp.where(some, den, 1.0)), MASKED)
    hi = lse.astype(BF).astype(F32)
    mid = (lse - hi).astype(BF).astype(F32)
    low = lse - hi - mid
    lane = lax.broadcasted_iota(jnp.int32, (n, 128), 1)
    stat = jnp.zeros((n, 128), F32)
    for h in range(2):
        rows = slice(h * n, (h + 1) * n)
        out_ref[0, :n, h * VDIM : (h + 1) * VDIM] = dot(
            att[rows], vu_ref[:, h * VDIM : (h + 1) * VDIM]
        ).astype(BF)
        for i, term in enumerate((hi, mid, low)):
            stat = jnp.where(lane == 3 * h + i, term[rows], stat)
    out_ref[0, n:, :VDIM] = stat.T[:STATS].astype(BF)
    out_ref[0, n:, VDIM:] = jnp.zeros((STATS, VDIM), BF)


def merge_kernel(got_ref, out_ref):
    m = got_ref.shape[0]
    n = out_ref.shape[0]
    stats = jnp.concatenate([got_ref[i, n:, :VDIM] for i in range(m)], axis=0).astype(F32).T
    for h in range(2):
        lse = []
        for i in range(m):
            at = i * STATS + 3 * h
            lse.append(stats[:, at : at + 1] + stats[:, at + 1 : at + 2] + stats[:, at + 2 : at + 3])
        top = functools.reduce(jnp.maximum, lse)
        den = jnp.zeros_like(top)
        acc = jnp.zeros((n, VDIM), F32)
        for i in range(m):
            w = jnp.exp(lse[i] - top)
            den = den + w
            acc = acc + w * got_ref[i, :n, h * VDIM : (h + 1) * VDIM].astype(F32)
        out_ref[:, h * VDIM : (h + 1) * VDIM] = (acc / den).astype(BF)


def finish_kernel(mix_ref, a_ref, b_ref, c_ref, d_ref, out_ref):
    total = a_ref[...].astype(F32) + b_ref[...].astype(F32) + c_ref[...].astype(F32) + d_ref[...].astype(F32)
    out_ref[...] = (mix_ref[...].astype(F32) + total).astype(BF)


def slots_kernel(ids_ref, gates_ref, oh_ref, hi_ref, lo_ref):
    experts = oh_ref.shape[0] // SLOTS
    n = oh_ref.shape[1]
    which = lax.broadcasted_iota(jnp.int32, (experts, n), 0)
    named = jnp.zeros((experts, n), F32)
    gate = jnp.zeros((experts, n), F32)
    for k in range(ids_ref.shape[0]):
        hit = which == ids_ref[k : k + 1, :]
        named = jnp.where(hit, 1.0, named)
        gate = jnp.where(hit, gates_ref[k : k + 1, :], gate)
    before = lax.broadcasted_iota(jnp.int32, (n, n), 0) < lax.broadcasted_iota(jnp.int32, (n, n), 1)
    count = dot(named.astype(BF), jnp.where(before, 1.0, 0.0).astype(BF))
    slot = jnp.where(named > 0.0, count, -1.0)
    ghi = gate.astype(BF).astype(F32)
    glo = gate - ghi
    level = lax.broadcasted_iota(jnp.int32, (SLOTS, n), 0).astype(F32)
    per = n // SLOTS
    for first in range(0, experts, per):
        parts = ([], [])
        for e in range(first, first + per):
            hit = slot[e : e + 1, :] == level
            oh_ref[e * SLOTS : (e + 1) * SLOTS, :] = jnp.where(hit, 1.0, 0.0).astype(BF)
            for part, v in zip(parts, (ghi, glo)):
                part.append(jnp.where(hit, v[e : e + 1, :], 0.0))
        for ref, part in zip((hi_ref, lo_ref), parts):
            ref[:, first * SLOTS : (first + per) * SLOTS] = jnp.concatenate(part, axis=0).T.astype(BF)


def dispatch_kernel(v0, v1, v2, v3, hid_ref, wo_ref, wa_ref, wb_ref, gain_ref, oh_ref, out_ref, mix_ref, in_ref, acc_ref):
    d = hid_ref.shape[1]
    w = wa_ref.shape[2]
    q = mix_ref.shape[1]
    x, _, _, c = my_place()
    t = lax.axis_index("tensor")

    @pl.when(pl.program_id(0) == 0)
    def _():
        first = v0[...]
        others = (v1[...], v2[...], v3[...])
        for i in range(NX):
            for b, ref in enumerate((wa_ref, wb_ref)):
                col = pl.multiple_of((lax.rem(x + i, NX) * NC + lax.rem(c + b, NC)) * w, w)
                total = dot(first, wo_ref[:, pl.ds(col, w)])
                for j, v in enumerate(others):
                    total = total + dot(v, ref[i * len(others) + j])
                acc_ref[:, pl.ds(col, w)] = (hid_ref[:, pl.ds(col, w)].astype(F32) + total).astype(BF)
        mix_ref[...] = acc_ref[:, pl.ds(pl.multiple_of(t * q, q), q)]
        mixed = acc_ref[...].astype(F32)
        scale = lax.rsqrt(jnp.sum(mixed * mixed, axis=-1, keepdims=True) / d + EPSILON)
        in_ref[...] = (mixed * scale * gain_ref[...]).astype(BF)

    out_ref[...] = dot(oh_ref[...], in_ref[...]).astype(BF)


def expert_kernel(x_ref, wgu_ref, wd_ref, out_ref):
    hid = wd_ref.shape[0]
    wide = wgu_ref.shape[1] // 2
    both = dot(x_ref[...], wgu_ref[...])
    gate, up = both[:, :wide], both[:, wide:]
    act = (gate / (1.0 + jnp.exp(-gate)) * up).astype(BF)[:, :hid]
    out_ref[...] = dot(act, wd_ref[...]).astype(BF)


def combine_kernel(place, rows_ref, hi_ref, lo_ref, out_ref):
    rows = rows_ref[...]
    out_ref[...] = (dot(hi_ref[...], rows) + dot(lo_ref[...], rows)).astype(BF)


def whole(n):
    return [pl.BlockSpec(memory_space=VM)] * n


def local(
    hidden, attn_gain, w_query, w_latent_down, kv_gain, w_key_up, w_value_up, w_out, ffn_gain,
    w_gate_exp, w_up_exp, w_down_exp, page_pool, page_table, request_group, suffix_lengths,
    token_order, expert_ids, expert_gates,
):
    seq_count = lax.axis_size("seq")
    tensor_count = lax.axis_size("tensor")
    tensor_index = lax.axis_index("tensor")
    n, d = hidden.shape
    quarter = d // tensor_count
    prefix = page_table.shape[1] * page_pool.shape[1]
    tok = token_order.reshape(seq_count, n)
    params = pltpu.CompilerParams(vmem_limit_bytes=56 << 20)
    large = pltpu.CompilerParams(vmem_limit_bytes=56 << 20)
    attend_params = pltpu.CompilerParams(vmem_limit_bytes=56 << 20)
    expert_params = pltpu.CompilerParams(vmem_limit_bytes=28 << 20)

    m = NZ * NY

    def spread(piece):
        got = [lax.ppermute(piece, "seq", seq_perm(i, 0, 0, 0)) for i in range(1, NX)]
        own = jnp.concatenate([piece] + got, axis=1)
        return own, lax.ppermute(own, "seq", seq_perm(0, 0, 0, 1))

    pages_a, pages_b = spread(page_pool[0].T)

    freq = ROPE_BASE ** (-2.0 * np.arange(ROPE // 2, dtype=np.float64) / ROPE)
    query, latent = pl.pallas_call(
        functools.partial(project_kernel, prefix),
        out_shape=(
            jax.ShapeDtypeStruct((m, n, w_query.shape[1]), BF),
            jax.ShapeDtypeStruct((KEY, n), BF),
        ),
        in_specs=[pl.BlockSpec(memory_space=SM)] + whole(8),
        out_specs=tuple(whole(2)),
        compiler_params=large,
        name="project",
    )(
        suffix_lengths, tok, jnp.asarray(freq[:, None], F32), jnp.asarray(np.tile(freq, 4)[None, :], F32), hidden,
        attn_gain.reshape(1, d), w_query, w_latent_down.T, kv_gain.reshape(1, LATENT),
    )

    lat_a, lat_b = spread(latent)
    queries = lax.all_to_all(query, "seq", 0, 0, tiled=True, axis_index_groups=zy_groups())

    x, _, _, c = my_place()
    share = d // (NX * NC)
    mine = lax.dynamic_slice_in_dim(w_out, (x * NC + c) * share, share, 1)
    other = jnp.stack([lax.ppermute(mine, "tensor", tensor_from(j, tensor_count)) for j in range(1, tensor_count)])
    wide = [other] + [lax.ppermute(other, "seq", seq_perm(i, 0, 0, 0)) for i in range(1, NX)]

    oh, ghi, glo = pl.pallas_call(
        slots_kernel,
        out_shape=(jax.ShapeDtypeStruct((seq_count * SLOTS, n), BF),)
        + (jax.ShapeDtypeStruct((n, seq_count * SLOTS), BF),) * 2,
        in_specs=whole(2),
        out_specs=tuple(whole(3)),
        compiler_params=params,
        name="slots",
    )(expert_ids.T, expert_gates.T)

    keys = NX * n

    def fixed(shape):
        return pl.BlockSpec(shape, lambda j, *_: (0,) * len(shape))

    partial = pl.pallas_call(
        attend_kernel,
        out_shape=jax.ShapeDtypeStruct((m, n + STATS, 2 * VDIM), BF),
        grid_spec=pltpu.PrefetchScalarGridSpec(
            num_scalar_prefetch=3,
            grid=(m,),
            in_specs=[fixed(tok.shape)]
            + [pl.BlockSpec((1,) + query.shape[1:], lambda j, *_: (j, 0, 0))]
            + [fixed((KEY, keys))] * 4
            + [fixed(w_key_up.shape), fixed(w_value_up.shape)],
            out_specs=pl.BlockSpec((1, n + STATS, 2 * VDIM), lambda j, *_: (j, 0, 0)),
            scratch_shapes=[
                pltpu.VMEM((2 * n, 4 * keys), F32),
                pltpu.VMEM((2 * n, KEY), BF),
                pltpu.SMEM((seq_count,), jnp.int32),
            ],
        ),
        compiler_params=attend_params,
        name="attend",
    )(
        suffix_lengths, request_group, page_table, tok, queries, pages_a, pages_b, lat_a, lat_b, w_key_up, w_value_up
    )

    got = lax.all_to_all(partial, "seq", 0, 0, tiled=True, axis_index_groups=zy_groups())
    values = pl.pallas_call(
        merge_kernel,
        out_shape=jax.ShapeDtypeStruct((n, 2 * VDIM), BF),
        in_specs=whole(1),
        out_specs=whole(1)[0],
        compiler_params=params,
        name="merge",
    )(got)
    all_values = [values] + [
        lax.ppermute(values, "tensor", tensor_from(j, tensor_count)) for j in range(1, tensor_count)
    ]
    wide, _ = lax.optimization_barrier((wide, values))
    wide = jnp.concatenate(wide, axis=0)
    wide_b = lax.ppermute(wide, "seq", seq_perm(0, 0, 0, 1))

    piece = jax.ShapeDtypeStruct((n, quarter), BF)
    rows = seq_count * SLOTS
    block = rows // 4
    outbound, mixed = pl.pallas_call(
        dispatch_kernel,
        out_shape=(pltpu.HBM((rows, d), BF), piece),
        grid=(rows // block,),
        in_specs=[fixed(values.shape)] * 4
        + [fixed(hidden.shape), fixed(w_out.shape), fixed(wide.shape), fixed(wide.shape), fixed((1, d))]
        + [pl.BlockSpec((block, n), lambda i: (i, 0))],
        out_specs=(pl.BlockSpec((block, d), lambda i: (i, 0)), fixed((n, quarter))),
        scratch_shapes=[pltpu.VMEM((n, d), BF), pltpu.VMEM((n, d), BF)],
        compiler_params=params,
        name="dispatch",
    )(*all_values, hidden, w_out, wide, wide_b, ffn_gain.reshape(1, d), oh)
    arrived = lax.all_to_all(outbound.reshape(seq_count, SLOTS, d), "seq", 0, 0, tiled=True)
    hid = w_gate_exp.shape[2]
    fill = jnp.zeros((d, -hid % 128), BF)
    both = jnp.concatenate([w_gate_exp[0], fill, w_up_exp[0], fill], axis=1)
    results = pl.pallas_call(
        expert_kernel,
        out_shape=pltpu.HBM((rows, d), BF),
        grid=(rows // block,),
        in_specs=[pl.BlockSpec((block, d), lambda i: (i, 0)), fixed(both.shape), fixed((hid, d))],
        out_specs=pl.BlockSpec((block, d), lambda i: (i, 0)),
        compiler_params=expert_params,
        name="expert",
    )(arrived.reshape(rows, d), both, w_down_exp[0])
    back = lax.all_to_all(results.reshape(seq_count, SLOTS, d), "seq", 0, 0, tiled=True)
    place = tensor_index.astype(jnp.int32).reshape(1)

    def combined(i):
        return pl.pallas_call(
            combine_kernel,
            out_shape=piece,
            grid_spec=pltpu.PrefetchScalarGridSpec(
                num_scalar_prefetch=1,
                grid=(1,),
                in_specs=[
                    pl.BlockSpec((rows, quarter), lambda j, place: (0, lax.rem(place[0] + i, tensor_count))),
                    fixed(ghi.shape),
                    fixed(glo.shape),
                ],
                out_specs=fixed((n, quarter)),
            ),
            compiler_params=params,
            name="combine",
        )(place, back.reshape(rows, d), ghi, glo)

    sums = [None] * tensor_count
    for i in (2, 1, 3):
        sums[i] = lax.ppermute(combined(i), "tensor", tensor_from(-i, tensor_count))
    sums[0] = combined(0)
    hidden_out = pl.pallas_call(
        finish_kernel, out_shape=piece, in_specs=whole(5), out_specs=whole(1)[0], compiler_params=expert_params, name="finish"
    )(mixed, *sums)
    width = KEY // tensor_count
    cache_part = lax.dynamic_slice_in_dim(latent, tensor_index * width, width, 0).T
    return (hidden_out, cache_part)


def solution(mesh):
    placed = (
        P("seq", None),
        P(),
        P(None, "tensor"),
        P(),
        P(),
        P(None, "tensor"),
        P(None, "tensor"),
        P("tensor", None),
        P(),
        P("seq", None, "tensor"),
        P("seq", None, "tensor"),
        P("seq", "tensor", None),
        P("seq", None, None),
        P(),
        P(),
        P(),
        P(),
        P("seq", None),
        P("seq", None),
    )

    return jax.shard_map(
        local,
        mesh=mesh,
        in_specs=placed,
        out_specs=(P("seq", "tensor"), P("seq", "tensor")),
        check_vma=False,
    )
```
